32 devices in a mesh: seq: 8 (over z, x), head: 4 (over y, core).
Axes of the slice: x: 2, y: 2, z: 4, core: 2. Of those that a mesh axis runs over, the one named last changes fastest.
Arguments:
- queries: bfloat16 [2048, 32, 128], P('seq', 'head'), may hold values from -6 to 6
- key_vectors: bfloat16 [2048, 4, 128], P(('seq', 'head')), may hold values from -6 to 6
- value_vectors: bfloat16 [2048, 4, 128], P(('seq', 'head')), may hold values from -6 to 6
- out_grad: bfloat16 [2048, 32, 128], P('seq', 'head'), may hold values from -6 to 6
Outputs:
- attended: bfloat16 [2048, 32, 128], P('seq', 'head')
- query_grad: bfloat16 [2048, 32, 128], P('seq', 'head')
- key_grad: bfloat16 [2048, 4, 128], P(('seq', 'head'))
- value_grad: bfloat16 [2048, 4, 128], P(('seq', 'head'))
The draws below stay inside these ranges and needn't reach their ends.
All inputs are finite; a program needn't handle non-finite values.
Results may differ from the reference program's by a relative error of at most 0.035.
Values may be sent and summed in bfloat16 or wider, within the bound.
A program may use at most 64 MiB of HBM per device.

```python
import math
import jax
import jax.numpy as jnp
from jax import lax

HEAD_DIM = 128
Q_PER_KV = 8
GROUPS = 4
KV_HEADS = 4
Q_HEADS = 32
TOKENS = 2048


def draw_queries(key, part):
    full_shape = (TOKENS, Q_HEADS, HEAD_DIM)
    own_key = jax.random.fold_in(key, 101)
    drawn = jnp.clip(jax.random.normal(own_key, full_shape, jnp.float32), -4.0, 4.0)
    return drawn.astype(jnp.bfloat16)


def draw_key_vectors(key, part):
    full_shape = (TOKENS, KV_HEADS, HEAD_DIM)
    own_key = jax.random.fold_in(key, 202)
    drawn = jnp.clip(jax.random.normal(own_key, full_shape, jnp.float32), -4.0, 4.0)
    return drawn.astype(jnp.bfloat16)


def shard_levels(stream_key, extent, pieces, smallest, top_value):
    factor_of, own = 1.0, jax.random.fold_in(stream_key, 6)
    for position, shards_of in pieces:
        draws = jnp.exp(jax.random.uniform(jax.random.fold_in(own, position), (shards_of,), jnp.float32, smallest / len(pieces), top_value / len(pieces)))
        factor_of = factor_of * jnp.repeat(draws, extent[position] // shards_of).reshape([-1 if axis == position else 1 for axis in range(len(extent))])
    return factor_of


def centred(rng, dims, deviation, reach, cuts=(), kind=jnp.bfloat16):
    values = jax.random.normal(rng, dims, jnp.float32) * deviation
    if len(cuts) > 0:
        values = shard_levels(rng, dims, cuts, -0.22, 0.18) * values
    return jnp.clip(values, min=-reach, max=reach).astype(kind)


def setup_inputs(seed: int = 0) -> dict:
    seeds = jax.random.split(jax.random.key(seed), 5)
    queries = draw_queries(jax.random.fold_in(seeds[4], 71), 0)
    key_vectors = draw_key_vectors(jax.random.fold_in(seeds[4], 71), 0)
    value_vectors = centred(seeds[2], (TOKENS, KV_HEADS, HEAD_DIM), 1.0, 6.0, ((0, 32),))
    out_grad = centred(seeds[3], (TOKENS, Q_HEADS, HEAD_DIM), 1.0, 6.0, ((0, 8), (1, 4)))
    return dict(queries=queries, key_vectors=key_vectors, value_vectors=value_vectors, out_grad=out_grad)


precise = lax.Precision.HIGHEST

def grouped_core(block):
    query_blk, key_blk, value_blk, grad_blk = block
    length = query_blk.shape[0]
    score_scale = 1.0 / math.sqrt(query_blk.shape[2])
    query_f = query_blk.astype(jnp.float32)
    key_f = key_blk.astype(jnp.float32)
    value_f = value_blk.astype(jnp.float32)
    grad_f = grad_blk.astype(jnp.float32)
    causal = jnp.arange(length, dtype=jnp.int32)[:, None] >= jnp.arange(length, dtype=jnp.int32)[None, :]
    scores = jnp.einsum('ihd,td->hit', query_f, key_f, precision=precise) * score_scale
    scores = jnp.where(causal[None], scores, -jnp.inf)
    row_max = lax.optimization_barrier(jnp.max(scores, axis=2))
    log_total = row_max + jnp.log(lax.optimization_barrier(jnp.sum(jnp.exp(scores - row_max[:, :, None]), axis=2)))
    prob_full = jnp.exp(scores - log_total[:, :, None])
    weights = prob_full.astype(jnp.bfloat16)
    attended = jnp.einsum('hit,td->ihd', weights.astype(jnp.float32), value_f, precision=precise).astype(jnp.bfloat16)
    delta_row = jnp.einsum('ihd,ihd->hi', grad_f, attended.astype(jnp.float32), precision=precise)
    prob_grad = jnp.einsum('ihd,td->hit', grad_f, value_f, precision=precise)
    score_grad = (prob_full * (prob_grad - delta_row[:, :, None])).astype(jnp.bfloat16)
    score_f = score_grad.astype(jnp.float32)
    query_grad = (jnp.einsum('hit,td->ihd', score_f, key_f, precision=precise) * score_scale).astype(jnp.bfloat16)
    key_grad = jnp.einsum('hit,ihd->td', score_f, query_f, precision=precise) * score_scale
    value_grad = jnp.einsum('hit,ihd->td', weights.astype(jnp.float32), grad_f, precision=precise)
    return (attended, query_grad, key_grad, value_grad)

def reference(queries, key_vectors, value_vectors, out_grad):
    tok_total = queries.shape[0]
    head_dim = queries.shape[2]
    kv_count = key_vectors.shape[1]
    group_len = tok_total // GROUPS
    half_heads = Q_PER_KV // 2
    attended_all = []
    query_all = []
    key_all = []
    value_all = []
    for kv_index in range(kv_count):
        first_head = kv_index * Q_PER_KV
        key_sum = jnp.zeros((tok_total, head_dim), jnp.float32)
        value_sum = jnp.zeros((tok_total, head_dim), jnp.float32)
        for shifted in range(2):
            offset = shifted * (group_len // 2)
            low_head = first_head + shifted * half_heads
            picked = (queries[:, low_head:low_head + half_heads], key_vectors[:, kv_index], value_vectors[:, kv_index], out_grad[:, low_head:low_head + half_heads])
            rolled = tuple((jnp.roll(member, -offset, axis=0).reshape((GROUPS, group_len) + member.shape[1:]) for member in picked))
            results = lax.map(grouped_core, rolled)
            unrolled = [jnp.roll(member.reshape((tok_total,) + member.shape[2:]), offset, axis=0) for member in results]
            attended_all.append(unrolled[0])
            query_all.append(unrolled[1])
            key_sum = key_sum + unrolled[2]
            value_sum = value_sum + unrolled[3]
        key_all.append(key_sum.astype(jnp.bfloat16))
        value_all.append(value_sum.astype(jnp.bfloat16))
    attended = jnp.concatenate(attended_all, axis=1)
    query_grad = jnp.concatenate(query_all, axis=1)
    key_grad = jnp.stack(key_all, axis=1)
    value_grad = jnp.stack(value_all, axis=1)
    return (attended, query_grad, key_grad, value_grad)
```

```python
import functools
import math

import jax
import jax.numpy as jnp
from jax import lax
from jax.experimental import pallas as pl
from jax.experimental.pallas import tpu as pltpu
from jax.sharding import PartitionSpec as P

GROUPS = 4


def shifted(value, axis, by):
    size = lax.axis_size(axis)
    return lax.ppermute(value, axis, [(i, (i + by) % size) for i in range(size)])


def visible(query_pos, key_pos, group_len, offset, tok_total):
    query_aligned = (query_pos - offset) % tok_total
    key_aligned = (key_pos - offset) % tok_total
    same_group = query_aligned[:, None] // group_len == key_aligned[None, :] // group_len
    return same_group & (key_aligned[None, :] <= query_aligned[:, None])


def per_device(queries, key_vectors, value_vectors, out_grad):
    key_home, value_home = (
        lax.all_to_all(key_vectors, "head", split_axis=1, concat_axis=0, tiled=True),
        lax.all_to_all(value_vectors, "head", split_axis=1, concat_axis=0, tiled=True),
    )
    key_home = key_home[:, 0, :]
    value_home = value_home[:, 0, :]
    tok_rows = queries.shape[0]
    half_heads = queries.shape[1] // 2
    head_dim = queries.shape[2]
    score_scale = 1.0 / math.sqrt(head_dim)
    devices = lax.axis_size("seq")
    group_span = devices // GROUPS
    tok_total = devices * tok_rows
    group_len = tok_total // GROUPS
    offsets = (0, group_len // 2)
    my_index = lax.axis_index("seq")
    local_pos = jnp.arange(tok_rows, dtype=jnp.int32)
    query_pos = my_index * tok_rows + local_pos
    q_parts = (queries[:, :half_heads], queries[:, half_heads:])
    grad_parts = (out_grad[:, :half_heads], out_grad[:, half_heads:])

    def key_positions(distance):
        return (my_index - distance) % devices * tok_rows + local_pos

    def scores_of(which_half, key_blk, allowed):
        scores = (
            jnp.einsum(
                "ihd,td->hit", q_parts[which_half], key_blk, preferred_element_type=jnp.float32
            )
            * score_scale
        )
        return jnp.where(allowed[None], scores, -jnp.inf)

    def forward_tile(states, key_blk, value_blk, distance):
        key_pos = key_positions(distance)
        updated = []
        for which_half in range(2):
            allowed = visible(query_pos, key_pos, group_len, offsets[which_half], tok_total)

            def forward_update(current, which_half=which_half, allowed=allowed):
                run_max, run_sum, running = current
                scores = scores_of(which_half, key_blk, allowed)
                new_max = jnp.maximum(run_max, jnp.max(scores, axis=2))
                weights = jnp.exp(scores - new_max[:, :, None])
                factor = jnp.exp(run_max - new_max)
                run_sum = run_sum * factor + jnp.sum(weights, axis=2)
                value_mix = jnp.einsum(
                    "hit,td->ihd",
                    weights.astype(jnp.bfloat16),
                    value_blk,
                    preferred_element_type=jnp.float32,
                )
                running = running * factor.T[:, :, None] + value_mix
                return (new_max, run_sum, running)

            updated.append(
                lax.cond(
                    jnp.any(allowed), forward_update, lambda current: current, states[which_half]
                )
            )
        return tuple(updated)

    def initial_state():
        return (
            jnp.full((half_heads, tok_rows), -jnp.inf, jnp.float32),
            jnp.zeros((half_heads, tok_rows), jnp.float32),
            jnp.zeros((tok_rows, half_heads, head_dim), jnp.float32),
        )

    forward_init = (initial_state(), initial_state())
    levels = (group_span - 1).bit_length()
    window_keys = key_home[None]
    window_values = value_home[None]
    for level_idx in range(levels):
        far_keys, far_values = shifted((window_keys, window_values), "seq", 2**level_idx)
        window_keys = jnp.concatenate([window_keys, far_keys], axis=0)
        window_values = jnp.concatenate([window_values, far_values], axis=0)

    def window_forward(distance, states):
        return forward_tile(states, window_keys[distance], window_values[distance], distance)

    states = lax.fori_loop(0, group_span, window_forward, forward_init)
    attended_parts = []
    log_totals = []
    deltas = []
    for which_half in range(2):
        run_max, run_sum, running = states[which_half]
        part_out = (running / run_sum.T[:, :, None]).astype(jnp.bfloat16)
        attended_parts.append(part_out)
        log_totals.append(run_max + jnp.log(run_sum))
        deltas.append(
            jnp.einsum(
                "ihd,ihd->hi", grad_parts[which_half], part_out, preferred_element_type=jnp.float32
            )
        )

    def backward_tile(current, key_blk, value_blk, distance):
        query_grads, key_acc, value_acc = current
        key_pos = key_positions(distance)
        new_query = []
        for which_half in range(2):
            allowed = visible(query_pos, key_pos, group_len, offsets[which_half], tok_total)

            def backward_update(inputs, which_half=which_half, allowed=allowed):
                query_acc, key_sum, value_sum = inputs
                scores = scores_of(which_half, key_blk, allowed)
                prob_full = jnp.exp(scores - log_totals[which_half][:, :, None])
                weights = prob_full.astype(jnp.bfloat16)
                prob_grad = jnp.einsum(
                    "ihd,td->hit",
                    grad_parts[which_half],
                    value_blk,
                    preferred_element_type=jnp.float32,
                )
                score_grad = (prob_full * (prob_grad - deltas[which_half][:, :, None])).astype(
                    jnp.bfloat16
                )
                query_acc = query_acc + jnp.einsum(
                    "hit,td->ihd", score_grad, key_blk, preferred_element_type=jnp.float32
                )
                key_sum = key_sum + jnp.einsum(
                    "hit,ihd->td",
                    score_grad,
                    q_parts[which_half],
                    preferred_element_type=jnp.float32,
                )
                value_sum = value_sum + jnp.einsum(
                    "hit,ihd->td",
                    weights,
                    grad_parts[which_half],
                    preferred_element_type=jnp.float32,
                )
                return (query_acc, key_sum, value_sum)

            query_acc, key_acc, value_acc = lax.cond(
                jnp.any(allowed),
                backward_update,
                lambda inputs: inputs,
                (query_grads[which_half], key_acc, value_acc),
            )
            new_query.append(query_acc)
        return (tuple(new_query), key_acc, value_acc)

    zero_query = jnp.zeros((tok_rows, half_heads, head_dim), jnp.float32)
    window_len = 2**levels
    key_buffer = jnp.zeros((window_len, tok_rows, head_dim), jnp.float32)
    value_buffer = jnp.zeros((window_len, tok_rows, head_dim), jnp.float32)

    def window_backward(distance, packed):
        query_grads, key_buffer, value_buffer = packed
        query_grads, key_acc, value_acc = backward_tile(
            (query_grads, key_buffer[distance], value_buffer[distance]),
            window_keys[distance],
            window_values[distance],
            distance,
        )
        key_buffer = lax.dynamic_update_index_in_dim(key_buffer, key_acc, distance, 0)
        value_buffer = lax.dynamic_update_index_in_dim(value_buffer, value_acc, distance, 0)
        return (query_grads, key_buffer, value_buffer)

    query_grads, key_buffer, value_buffer = lax.fori_loop(
        0, group_span, window_backward, ((zero_query, zero_query), key_buffer, value_buffer)
    )
    for level_idx in reversed(range(levels)):
        reach_len = 2**level_idx
        far_keys, far_values = (
            shifted(
                key_buffer[reach_len : 2 * reach_len].astype(jnp.bfloat16), "seq", -reach_len
            ).astype(jnp.float32),
            shifted(
                value_buffer[reach_len : 2 * reach_len].astype(jnp.bfloat16), "seq", -reach_len
            ).astype(jnp.float32),
        )
        key_buffer = key_buffer[:reach_len] + far_keys
        value_buffer = value_buffer[:reach_len] + far_values
    key_acc = key_buffer[0]
    value_acc = value_buffer[0]
    attended = jnp.concatenate(attended_parts, axis=1)
    query_grad = (jnp.concatenate(query_grads, axis=1) * score_scale).astype(jnp.bfloat16)
    key_home_grad = (key_acc * score_scale).astype(jnp.bfloat16)[:, None, :]
    value_home_grad = value_acc.astype(jnp.bfloat16)[:, None, :]
    key_grad, value_grad = (
        lax.all_to_all(key_home_grad, "head", split_axis=0, concat_axis=1, tiled=True),
        lax.all_to_all(value_home_grad, "head", split_axis=0, concat_axis=1, tiled=True),
    )
    return (attended, query_grad, key_grad, value_grad)


def pair_groups(devices, head_devices, sizes):
    _, kv_rows, kv_heads, head_dim = sizes
    return devices == 2 * GROUPS and kv_heads == head_devices and head_dim == 128


NT = (((1,), (1,)), ((), ()))
NN = (((1,), (0,)), ((), ()))


def dot(left, right, dims=NN):
    return lax.dot_general(left, right, dims, preferred_element_type=jnp.float32)


def fused_kernel(
    devices,
    peers,
    heads,
    q_hbm,
    k_ref,
    v_ref,
    g_hbm,
    att_hbm,
    dq_hbm,
    dk_ref,
    dv_ref,
    q_ref,
    g_ref,
    att_ref,
    dq_ref,
    spread,
    kv_send,
    kv,
    kv_t,
    w_ref,
    ds_ref,
    g_send,
    g_land,
    load_sem,
    store_sem,
    kv_send_sem,
    kv_recv_sem,
    g_send_sem,
    g_recv_sem,
):
    s = lax.axis_index("seq")
    h = lax.axis_index("head")
    after = lax.rem(s + 1, devices)
    before = lax.rem(s + devices - 1, devices)
    rows = q_ref.shape[0]
    head_dim = q_ref.shape[1]
    tokens = rows // heads
    piece = tokens // peers
    chunk = 256
    chunk_tok = chunk // heads
    chunks = rows // chunk
    scale = 1.0 / math.sqrt(head_dim)
    log2e = 1.4426950408889634

    def peer(d):
        return lax.rem(h + d, peers)

    barrier = pltpu.get_barrier_semaphore()
    for d in range(peers):
        if d:
            pl.semaphore_signal(barrier, inc=1, device_id=(s, peer(d)), device_id_type=MESH)
        pl.semaphore_signal(barrier, inc=1, device_id=(after, peer(d)), device_id_type=MESH)
        pl.semaphore_signal(barrier, inc=1, device_id=(before, peer(d)), device_id_type=MESH)

    load_q = pltpu.make_async_copy(q_hbm, q_ref, load_sem.at[0])
    load_g = pltpu.make_async_copy(g_hbm, g_ref, load_sem.at[1])
    load_q.start()
    load_g.start()

    spread[0] = k_ref[...].astype(jnp.float32)
    spread[1] = v_ref[...].astype(jnp.float32)
    for p in range(peers):
        for which in range(2):
            kv_send[p, which] = spread[which, pl.ds(p, piece, stride=peers), :].astype(jnp.bfloat16)

    mine = pl.ds(pl.multiple_of(h * piece, piece), piece)
    mine_own = pl.ds(pl.multiple_of(tokens + h * piece, piece), piece)
    pl.semaphore_wait(barrier, 3 * peers - 1)

    own_copies = []
    prev_copies = []
    for d in range(1, peers):
        own_copies.append(
            pltpu.make_async_remote_copy(
                src_ref=kv_send.at[peer(d)],
                dst_ref=kv.at[:, mine_own, :],
                send_sem=kv_send_sem.at[d],
                recv_sem=kv_recv_sem.at[d],
                device_id=(s, peer(d)),
                device_id_type=MESH,
            )
        )
    for d in range(peers):
        prev_copies.append(
            pltpu.make_async_remote_copy(
                src_ref=kv_send.at[peer(d)],
                dst_ref=kv.at[:, mine, :],
                send_sem=kv_send_sem.at[peers + d],
                recv_sem=kv_recv_sem.at[peers + d],
                device_id=(after, peer(d)),
                device_id_type=MESH,
            )
        )
    for copy in own_copies + prev_copies:
        copy.start()
    kv[:, mine_own, :] = kv_send[h]
    for copy in own_copies + prev_copies:
        copy.wait()
    load_q.wait()
    load_g.wait()

    for which in range(2):
        kv_t[which] = kv[which].T

    lane = lax.broadcasted_iota(jnp.int32, (1, chunk), 1)
    sees_prev = (lax.rem(lane, heads) // (heads // 2)) == lax.rem(s + 1, 2)
    diag_key = lax.broadcasted_iota(jnp.int32, (chunk_tok, chunk), 0)
    diag_tok = lax.broadcasted_iota(jnp.int32, (chunk_tok, chunk), 1) // heads
    diag = diag_key <= diag_tok
    unit = scale * log2e

    for a in range(chunks):
        here = pl.ds(a * chunk, chunk)
        own_keys = chunk_tok * (a + 1)
        total_keys = tokens + own_keys
        q_a = q_ref[here, :]
        g_a = g_ref[here, :]
        scores = dot(kv[0, :total_keys, :], q_a, NT) * unit
        prev = scores[:tokens]
        full = scores[tokens : total_keys - chunk_tok]
        edge = jnp.where(diag, scores[total_keys - chunk_tok :], -jnp.inf)
        top = jnp.where(sees_prev, jnp.max(prev, axis=0, keepdims=True), -jnp.inf)
        top = jnp.maximum(top, jnp.max(edge, axis=0, keepdims=True))
        if a:
            top = jnp.maximum(top, jnp.max(full, axis=0, keepdims=True))
        top_prev = jnp.where(sees_prev, top, 1e30)
        parts = [jnp.exp2(prev - top_prev)]
        if a:
            parts.append(jnp.exp2(full - top))
        parts.append(jnp.exp2(edge - top))
        probs = jnp.concatenate(parts, axis=0)
        inverse = 1.0 / jnp.sum(probs, axis=0, keepdims=True)
        probs = probs * inverse
        w_ref[:total_keys, here] = probs.astype(jnp.bfloat16)
        prob_grad = dot(kv[1, :total_keys, :], g_a, NT)
        delta = jnp.sum(probs * prob_grad, axis=0, keepdims=True)
        ds_ref[:total_keys, here] = (probs * (prob_grad - delta)).astype(jnp.bfloat16)
        limit = tokens + -(-own_keys // 128) * 128
        if limit > total_keys:
            blank = jnp.zeros((limit - total_keys, chunk), jnp.bfloat16)
            w_ref[total_keys:limit, here] = blank
            ds_ref[total_keys:limit, here] = blank

    def send_grads(which, slot, target, d):
        return pltpu.make_async_remote_copy(
            src_ref=g_send.at[which, :, pl.ds(pl.multiple_of(peer(d) * piece, piece), piece), :],
            dst_ref=g_land.at[which, h],
            send_sem=g_send_sem.at[slot],
            recv_sem=g_recv_sem.at[slot],
            device_id=(target, peer(d)),
            device_id_type=MESH,
        )

    g_send[0, 1] = dot(w_ref[:tokens, :], g_ref[...]).astype(jnp.bfloat16)
    g_send[0, 0] = (dot(ds_ref[:tokens, :], q_ref[...]) * scale).astype(jnp.bfloat16)
    grad_copies = [send_grads(0, peers + d, before, d) for d in range(peers)]
    for copy in grad_copies:
        copy.start()

    for low in range(0, tokens, 128):
        keys = slice(tokens + low, tokens + low + 128)
        first = low * heads
        g_send[1, 1, low : low + 128] = dot(w_ref[keys, first:], g_ref[first:, :]).astype(jnp.bfloat16)
        g_send[1, 0, low : low + 128] = (dot(ds_ref[keys, first:], q_ref[first:, :]) * scale).astype(
            jnp.bfloat16
        )
    own_grads = [send_grads(1, d, s, d) for d in range(1, peers)]
    for copy in own_grads:
        copy.start()
    g_land[1, h] = g_send[1, :, mine, :]

    stores = []
    for a in range(chunks):
        here = pl.ds(a * chunk, chunk)
        limit = tokens + -(-(chunk_tok * (a + 1)) // 128) * 128
        att_ref[here, :] = dot(kv_t[1, :, :limit], w_ref[:limit, here]).astype(jnp.bfloat16).T
        dq_ref[here, :] = (dot(kv_t[0, :, :limit], ds_ref[:limit, here]) * scale).astype(jnp.bfloat16).T
    stores = [
        pltpu.make_async_copy(att_ref, att_hbm, store_sem.at[0]),
        pltpu.make_async_copy(dq_ref, dq_hbm, store_sem.at[1]),
    ]
    for copy in stores:
        copy.start()

    for copy in grad_copies + own_grads:
        copy.wait()
    for which, out in ((0, dk_ref), (1, dv_ref)):
        for p in range(peers):
            spread[which, pl.ds(p, piece, stride=peers), :] = g_land[0, p, which].astype(
                jnp.float32
            ) + g_land[1, p, which].astype(jnp.float32)
        out[...] = spread[which].astype(jnp.bfloat16)
    for copy in stores:
        copy.wait()


MESH = pl.DeviceIdType.MESH


def fused_device(queries, key_vectors, value_vectors, out_grad):
    devices = lax.axis_size("seq")
    peers = lax.axis_size("head")
    tokens, heads, head_dim = queries.shape
    piece, kv_heads, _ = key_vectors.shape
    rows = tokens * heads
    kv_rows = piece * kv_heads
    bf16, f32 = jnp.bfloat16, jnp.float32
    big = jax.ShapeDtypeStruct((rows, head_dim), bf16)
    small = jax.ShapeDtypeStruct((kv_rows, head_dim), bf16)
    hbm = pl.BlockSpec(memory_space=pl.ANY)
    vmem = pl.BlockSpec(memory_space=pltpu.VMEM)
    dma = pltpu.SemaphoreType.DMA
    att, dq, dk, dv = pl.pallas_call(
        functools.partial(fused_kernel, devices, peers, heads),
        out_shape=(big, big, small, small),
        in_specs=[hbm, vmem, vmem, hbm],
        out_specs=(hbm, hbm, vmem, vmem),
        scratch_shapes=[
            pltpu.VMEM((rows, head_dim), bf16),
            pltpu.VMEM((rows, head_dim), bf16),
            pltpu.VMEM((rows, head_dim), bf16),
            pltpu.VMEM((rows, head_dim), bf16),
            pltpu.VMEM((2, kv_rows, head_dim), f32),
            pltpu.VMEM((peers, 2, piece, head_dim), bf16),
            pltpu.VMEM((2, 2 * tokens, head_dim), bf16),
            pltpu.VMEM((2, head_dim, 2 * tokens), bf16),
            pltpu.VMEM((2 * tokens, rows), bf16),
            pltpu.VMEM((2 * tokens, rows), bf16),
            pltpu.VMEM((2, 2, tokens, head_dim), bf16),
            pltpu.VMEM((2, peers, 2, piece, head_dim), bf16),
            dma((2,)),
            dma((2,)),
            dma((2 * peers,)),
            dma((2 * peers,)),
            dma((2 * peers,)),
            dma((2 * peers,)),
        ],
        compiler_params=pltpu.CompilerParams(
            collective_id=0, has_side_effects=True, vmem_limit_bytes=48 * 1024 * 1024
        ),
    )(
        queries.reshape(rows, head_dim),
        key_vectors.reshape(kv_rows, head_dim),
        value_vectors.reshape(kv_rows, head_dim),
        out_grad.reshape(rows, head_dim),
    )
    return (
        att.reshape(queries.shape),
        dq.reshape(queries.shape),
        dk.reshape(key_vectors.shape),
        dv.reshape(value_vectors.shape),
    )


def solution(mesh):
    def step(queries, key_vectors, value_vectors, out_grad):
        sizes = (queries.shape[0], queries.shape[1], key_vectors.shape[1], queries.shape[2])
        body = fused_device if pair_groups(mesh.shape["seq"], mesh.shape["head"], sizes) else per_device
        return run(body)(queries, key_vectors, value_vectors, out_grad)

    run = lambda body: jax.shard_map(
        body,
        mesh=mesh,
        in_specs=(
            P("seq", "head", None),
            P(("seq", "head"), None, None),
            P(("seq", "head"), None, None),
            P("seq", "head", None),
        ),
        out_specs=(
            P("seq", "head", None),
            P("seq", "head", None),
            P(("seq", "head"), None, None),
            P(("seq", "head"), None, None),
        ),
        check_vma=False,
    )
    return step
```

```python
import functools
import math

import jax
import jax.numpy as jnp
from jax import lax
from jax.experimental import pallas as pl
from jax.experimental.pallas import tpu as pltpu
from jax.sharding import PartitionSpec as P

GROUPS = 4


def shifted(value, axis, by):
    size = lax.axis_size(axis)
    return lax.ppermute(value, axis, [(i, (i + by) % size) for i in range(size)])


def visible(query_pos, key_pos, group_len, offset, tok_total):
    query_aligned = (query_pos - offset) % tok_total
    key_aligned = (key_pos - offset) % tok_total
    same_group = query_aligned[:, None] // group_len == key_aligned[None, :] // group_len
    return same_group & (key_aligned[None, :] <= query_aligned[:, None])


def per_device(queries, key_vectors, value_vectors, out_grad):
    key_home, value_home = (
        lax.all_to_all(key_vectors, "head", split_axis=1, concat_axis=0, tiled=True),
        lax.all_to_all(value_vectors, "head", split_axis=1, concat_axis=0, tiled=True),
    )
    key_home = key_home[:, 0, :]
    value_home = value_home[:, 0, :]
    tok_rows = queries.shape[0]
    half_heads = queries.shape[1] // 2
    head_dim = queries.shape[2]
    score_scale = 1.0 / math.sqrt(head_dim)
    devices = lax.axis_size("seq")
    group_span = devices // GROUPS
    tok_total = devices * tok_rows
    group_len = tok_total // GROUPS
    offsets = (0, group_len // 2)
    my_index = lax.axis_index("seq")
    local_pos = jnp.arange(tok_rows, dtype=jnp.int32)
    query_pos = my_index * tok_rows + local_pos
    q_parts = (queries[:, :half_heads], queries[:, half_heads:])
    grad_parts = (out_grad[:, :half_heads], out_grad[:, half_heads:])

    def key_positions(distance):
        return (my_index - distance) % devices * tok_rows + local_pos

    def scores_of(which_half, key_blk, allowed):
        scores = (
            jnp.einsum(
                "ihd,td->hit", q_parts[which_half], key_blk, preferred_element_type=jnp.float32
            )
            * score_scale
        )
        return jnp.where(allowed[None], scores, -jnp.inf)

    def forward_tile(states, key_blk, value_blk, distance):
        key_pos = key_positions(distance)
        updated = []
        for which_half in range(2):
            allowed = visible(query_pos, key_pos, group_len, offsets[which_half], tok_total)

            def forward_update(current, which_half=which_half, allowed=allowed):
                run_max, run_sum, running = current
                scores = scores_of(which_half, key_blk, allowed)
                new_max = jnp.maximum(run_max, jnp.max(scores, axis=2))
                weights = jnp.exp(scores - new_max[:, :, None])
                factor = jnp.exp(run_max - new_max)
                run_sum = run_sum * factor + jnp.sum(weights, axis=2)
                value_mix = jnp.einsum(
                    "hit,td->ihd",
                    weights.astype(jnp.bfloat16),
                    value_blk,
                    preferred_element_type=jnp.float32,
                )
                running = running * factor.T[:, :, None] + value_mix
                return (new_max, run_sum, running)

            updated.append(
                lax.cond(
                    jnp.any(allowed), forward_update, lambda current: current, states[which_half]
                )
            )
        return tuple(updated)

    def initial_state():
        return (
            jnp.full((half_heads, tok_rows), -jnp.inf, jnp.float32),
            jnp.zeros((half_heads, tok_rows), jnp.float32),
            jnp.zeros((tok_rows, half_heads, head_dim), jnp.float32),
        )

    forward_init = (initial_state(), initial_state())
    levels = (group_span - 1).bit_length()
    window_keys = key_home[None]
    window_values = value_home[None]
    for level_idx in range(levels):
        far_keys, far_values = shifted((window_keys, window_values), "seq", 2**level_idx)
        window_keys = jnp.concatenate([window_keys, far_keys], axis=0)
        window_values = jnp.concatenate([window_values, far_values], axis=0)

    def window_forward(distance, states):
        return forward_tile(states, window_keys[distance], window_values[distance], distance)

    states = lax.fori_loop(0, group_span, window_forward, forward_init)
    attended_parts = []
    log_totals = []
    deltas = []
    for which_half in range(2):
        run_max, run_sum, running = states[which_half]
        part_out = (running / run_sum.T[:, :, None]).astype(jnp.bfloat16)
        attended_parts.append(part_out)
        log_totals.append(run_max + jnp.log(run_sum))
        deltas.append(
            jnp.einsum(
                "ihd,ihd->hi", grad_parts[which_half], part_out, preferred_element_type=jnp.float32
            )
        )

    def backward_tile(current, key_blk, value_blk, distance):
        query_grads, key_acc, value_acc = current
        key_pos = key_positions(distance)
        new_query = []
        for which_half in range(2):
            allowed = visible(query_pos, key_pos, group_len, offsets[which_half], tok_total)

            def backward_update(inputs, which_half=which_half, allowed=allowed):
                query_acc, key_sum, value_sum = inputs
                scores = scores_of(which_half, key_blk, allowed)
                prob_full = jnp.exp(scores - log_totals[which_half][:, :, None])
                weights = prob_full.astype(jnp.bfloat16)
                prob_grad = jnp.einsum(
                    "ihd,td->hit",
                    grad_parts[which_half],
                    value_blk,
                    preferred_element_type=jnp.float32,
                )
                score_grad = (prob_full * (prob_grad - deltas[which_half][:, :, None])).astype(
                    jnp.bfloat16
                )
                query_acc = query_acc + jnp.einsum(
                    "hit,td->ihd", score_grad, key_blk, preferred_element_type=jnp.float32
                )
                key_sum = key_sum + jnp.einsum(
                    "hit,ihd->td",
                    score_grad,
                    q_parts[which_half],
                    preferred_element_type=jnp.float32,
                )
                value_sum = value_sum + jnp.einsum(
                    "hit,ihd->td",
                    weights,
                    grad_parts[which_half],
                    preferred_element_type=jnp.float32,
                )
                return (query_acc, key_sum, value_sum)

            query_acc, key_acc, value_acc = lax.cond(
                jnp.any(allowed),
                backward_update,
                lambda inputs: inputs,
                (query_grads[which_half], key_acc, value_acc),
            )
            new_query.append(query_acc)
        return (tuple(new_query), key_acc, value_acc)

    zero_query = jnp.zeros((tok_rows, half_heads, head_dim), jnp.float32)
    window_len = 2**levels
    key_buffer = jnp.zeros((window_len, tok_rows, head_dim), jnp.float32)
    value_buffer = jnp.zeros((window_len, tok_rows, head_dim), jnp.float32)

    def window_backward(distance, packed):
        query_grads, key_buffer, value_buffer = packed
        query_grads, key_acc, value_acc = backward_tile(
            (query_grads, key_buffer[distance], value_buffer[distance]),
            window_keys[distance],
            window_values[distance],
            distance,
        )
        key_buffer = lax.dynamic_update_index_in_dim(key_buffer, key_acc, distance, 0)
        value_buffer = lax.dynamic_update_index_in_dim(value_buffer, value_acc, distance, 0)
        return (query_grads, key_buffer, value_buffer)

    query_grads, key_buffer, value_buffer = lax.fori_loop(
        0, group_span, window_backward, ((zero_query, zero_query), key_buffer, value_buffer)
    )
    for level_idx in reversed(range(levels)):
        reach_len = 2**level_idx
        far_keys, far_values = (
            shifted(
                key_buffer[reach_len : 2 * reach_len].astype(jnp.bfloat16), "seq", -reach_len
            ).astype(jnp.float32),
            shifted(
                value_buffer[reach_len : 2 * reach_len].astype(jnp.bfloat16), "seq", -reach_len
            ).astype(jnp.float32),
        )
        key_buffer = key_buffer[:reach_len] + far_keys
        value_buffer = value_buffer[:reach_len] + far_values
    key_acc = key_buffer[0]
    value_acc = value_buffer[0]
    attended = jnp.concatenate(attended_parts, axis=1)
    query_grad = (jnp.concatenate(query_grads, axis=1) * score_scale).astype(jnp.bfloat16)
    key_home_grad = (key_acc * score_scale).astype(jnp.bfloat16)[:, None, :]
    value_home_grad = value_acc.astype(jnp.bfloat16)[:, None, :]
    key_grad, value_grad = (
        lax.all_to_all(key_home_grad, "head", split_axis=0, concat_axis=1, tiled=True),
        lax.all_to_all(value_home_grad, "head", split_axis=0, concat_axis=1, tiled=True),
    )
    return (attended, query_grad, key_grad, value_grad)


def pair_groups(devices, head_devices, sizes):
    _, kv_rows, kv_heads, head_dim = sizes
    return devices == 2 * GROUPS and kv_heads == head_devices and head_dim == 128


NT = (((1,), (1,)), ((), ()))
NN = (((1,), (0,)), ((), ()))


def dot(left, right, dims=NN):
    return lax.dot_general(left, right, dims, preferred_element_type=jnp.float32)


def fused_kernel(
    devices,
    peers,
    heads,
    q_hbm,
    k_hbm,
    v_hbm,
    g_hbm,
    att_ref,
    dq_ref,
    dk_ref,
    dv_ref,
    q_ref,
    g_ref,
    kv_in,
    spread,
    kv_send,
    kv,
    kv_t,
    p_own,
    dp_own,
    stats,
    w_ref,
    ds_ref,
    g_send,
    g_land,
    load_sem,
    kv_send_sem,
    kv_recv_sem,
    g_send_sem,
    g_recv_sem,
):
    s = lax.axis_index("seq")
    h = lax.axis_index("head")
    after = lax.rem(s + 1, devices)
    before = lax.rem(s + devices - 1, devices)
    rows = q_ref.shape[0]
    head_dim = q_ref.shape[1]
    tokens = rows // heads
    piece = tokens // peers
    chunk = 256
    chunk_tok = chunk // heads
    chunks = rows // chunk
    scale = 1.0 / math.sqrt(head_dim)
    unit = scale * 1.4426950408889634

    def peer(d):
        return lax.rem(h + d, peers)

    loads = [
        pltpu.make_async_copy(src, dst, load_sem.at[i])
        for i, (src, dst) in enumerate(
            ((k_hbm, kv_in.at[0]), (v_hbm, kv_in.at[1]), (q_hbm, q_ref), (g_hbm, g_ref))
        )
    ]
    for copy in loads:
        copy.start()

    barrier = pltpu.get_barrier_semaphore()
    for d in range(peers):
        pl.semaphore_signal(barrier, inc=1, device_id=(before, peer(d)), device_id_type=MESH)
        pl.semaphore_signal(barrier, inc=1, device_id=(after, peer(d)), device_id_type=MESH)
        if d:
            pl.semaphore_signal(barrier, inc=1, device_id=(s, peer(d)), device_id_type=MESH)

    for which in range(2):
        loads[which].wait()
        spread[which] = kv_in[which].astype(jnp.float32)
        for p in range(peers):
            kv_send[p, which] = spread[which, pl.ds(p, piece, stride=peers), :].astype(jnp.bfloat16)

    mine = pl.ds(pl.multiple_of(h * piece, piece), piece)
    mine_own = pl.ds(pl.multiple_of(tokens + h * piece, piece), piece)
    pl.semaphore_wait(barrier, 3 * peers - 1)

    def send_kv(slot, src, dst, target, d):
        return pltpu.make_async_remote_copy(
            src_ref=src,
            dst_ref=dst,
            send_sem=kv_send_sem.at[slot],
            recv_sem=kv_recv_sem.at[slot],
            device_id=(target, peer(d)),
            device_id_type=MESH,
        )

    own_copies = [
        send_kv(d, kv_send.at[peer(d)], kv.at[:, mine_own, :], s, d) for d in range(1, peers)
    ]
    prev_copies = [
        [
            send_kv(
                (1 + which) * peers + d, kv_send.at[peer(d), which], kv.at[which, mine, :], after, d
            )
            for d in range(peers)
        ]
        for which in range(2)
    ]
    for copy in own_copies + prev_copies[0] + prev_copies[1]:
        copy.start()
    kv[:, mine_own, :] = kv_send[h]
    loads[2].wait()
    loads[3].wait()
    for copy in own_copies:
        copy.wait()

    lane = lax.broadcasted_iota(jnp.int32, (1, chunk), 1)
    sees_prev = (lax.rem(lane, heads) // (heads // 2)) == lax.rem(s + 1, 2)
    diag_key = lax.broadcasted_iota(jnp.int32, (chunk_tok, chunk), 0)
    diag_tok = lax.broadcasted_iota(jnp.int32, (chunk_tok, chunk), 1) // heads
    diag = diag_key <= diag_tok

    for a in range(chunks):
        here = pl.ds(a * chunk, chunk)
        own_keys = chunk_tok * (a + 1)
        inner = own_keys - chunk_tok
        scores = dot(kv[0, tokens : tokens + own_keys, :], q_ref[here, :], NT) * unit
        edge = jnp.where(diag, scores[inner:], -jnp.inf)
        top = jnp.max(edge, axis=0, keepdims=True)
        if a:
            top = jnp.maximum(top, jnp.max(scores[:inner], axis=0, keepdims=True))
            edge = jnp.concatenate([scores[:inner], edge], axis=0)
        probs = jnp.exp2(edge - top)
        prob_grad = dot(kv[1, tokens : tokens + own_keys, :], g_ref[here, :], NT)
        p_own[:own_keys, here] = probs
        dp_own[:own_keys, here] = prob_grad
        stats[0:1, here] = top
        stats[1:2, here] = jnp.sum(probs, axis=0, keepdims=True)
        stats[2:3, here] = jnp.sum(probs * prob_grad, axis=0, keepdims=True)

    def send_grads(block, which, slot, target, d):
        return pltpu.make_async_remote_copy(
            src_ref=g_send.at[block, which, pl.ds(pl.multiple_of(peer(d) * piece, piece), piece), :],
            dst_ref=g_land.at[block, h, which],
            send_sem=g_send_sem.at[slot],
            recv_sem=g_recv_sem.at[slot],
            device_id=(target, peer(d)),
            device_id_type=MESH,
        )

    for copy in prev_copies[0]:
        copy.wait()
    for a in range(chunks):
        here = pl.ds(a * chunk, chunk)
        scores = dot(kv[0, :tokens, :], q_ref[here, :], NT) * unit
        top_own = stats[0:1, here]
        top = jnp.where(sees_prev, jnp.max(scores, axis=0, keepdims=True), -jnp.inf)
        top = jnp.maximum(top, top_own)
        probs = jnp.exp2(scores - jnp.where(sees_prev, top, 1e30))
        factor = jnp.exp2(top_own - top)
        inverse = 1.0 / (jnp.sum(probs, axis=0, keepdims=True) + factor * stats[1:2, here])
        w_ref[:tokens, here] = (probs * inverse).astype(jnp.bfloat16)
        stats[3:4, here] = factor * inverse
    g_send[0, 1] = dot(w_ref[:tokens, :], g_ref[...]).astype(jnp.bfloat16)
    prev_v_grads = [send_grads(0, 1, peers + d, before, d) for d in range(peers)]
    for copy in prev_v_grads:
        copy.start()

    for copy in prev_copies[1]:
        copy.wait()
    for a in range(chunks):
        here = pl.ds(a * chunk, chunk)
        weights = w_ref[:tokens, here].astype(jnp.float32)
        prob_grad = dot(kv[1, :tokens, :], g_ref[here, :], NT)
        delta = jnp.sum(weights * prob_grad, axis=0, keepdims=True) + stats[3:4, here] * stats[2:3, here]
        stats[4:5, here] = delta
        ds_ref[:tokens, here] = (weights * (prob_grad - delta)).astype(jnp.bfloat16)
    g_send[0, 0] = (dot(ds_ref[:tokens, :], q_ref[...]) * scale).astype(jnp.bfloat16)
    prev_k_grads = [send_grads(0, 0, d, before, d) for d in range(peers)]
    for copy in prev_k_grads:
        copy.start()

    for a in range(chunks):
        here = pl.ds(a * chunk, chunk)
        own_keys = chunk_tok * (a + 1)
        weights = p_own[:own_keys, here] * stats[3:4, here]
        w_ref[tokens : tokens + own_keys, here] = weights.astype(jnp.bfloat16)
        ds_ref[tokens : tokens + own_keys, here] = (
            weights * (dp_own[:own_keys, here] - stats[4:5, here])
        ).astype(jnp.bfloat16)
        limit = -(-own_keys // 128) * 128
        if limit > own_keys:
            blank = jnp.zeros((limit - own_keys, chunk), jnp.bfloat16)
            w_ref[tokens + own_keys : tokens + limit, here] = blank
            ds_ref[tokens + own_keys : tokens + limit, here] = blank
    for low in range(0, tokens, 128):
        keys = slice(tokens + low, tokens + low + 128)
        first = low * heads
        g_send[1, 1, low : low + 128] = dot(w_ref[keys, first:], g_ref[first:, :]).astype(jnp.bfloat16)
        g_send[1, 0, low : low + 128] = (dot(ds_ref[keys, first:], q_ref[first:, :]) * scale).astype(
            jnp.bfloat16
        )
    own_grads = [
        send_grads(1, which, (2 + which) * peers + d, s, d)
        for which in range(2)
        for d in range(1, peers)
    ]
    for copy in own_grads:
        copy.start()
    g_land[1, h] = g_send[1, :, mine, :]

    for which in range(2):
        kv_t[which] = kv[which].T
    for a in range(chunks):
        here = pl.ds(a * chunk, chunk)
        limit = tokens + -(-(chunk_tok * (a + 1)) // 128) * 128
        att_ref[here, :] = dot(kv_t[1, :, :limit], w_ref[:limit, here]).astype(jnp.bfloat16).T
        dq_ref[here, :] = (dot(kv_t[0, :, :limit], ds_ref[:limit, here]) * scale).astype(jnp.bfloat16).T

    for copy in prev_v_grads + prev_k_grads + own_grads:
        copy.wait()
    for which, out in ((0, dk_ref), (1, dv_ref)):
        for p in range(peers):
            spread[which, pl.ds(p, piece, stride=peers), :] = g_land[0, p, which].astype(
                jnp.float32
            ) + g_land[1, p, which].astype(jnp.float32)
        out[...] = spread[which].astype(jnp.bfloat16)


def place_kernel(*refs):
    count = (len(refs) - 1) // 2
    copies = [
        pltpu.make_async_copy(refs[i], refs[count + i], refs[-1].at[i]) for i in range(count)
    ]
    for copy in copies:
        copy.start()
    for copy in copies:
        copy.wait()


MESH = pl.DeviceIdType.MESH


def fused_device(queries, key_vectors, value_vectors, out_grad):
    devices = lax.axis_size("seq")
    peers = lax.axis_size("head")
    tokens, heads, head_dim = queries.shape
    piece, kv_heads, _ = key_vectors.shape
    rows = tokens * heads
    kv_rows = piece * kv_heads
    bf16, f32 = jnp.bfloat16, jnp.float32
    big = jax.ShapeDtypeStruct((rows, head_dim), bf16)
    small = jax.ShapeDtypeStruct((kv_rows, head_dim), bf16)
    hbm = pl.BlockSpec(memory_space=pltpu.HBM)
    vmem = pl.BlockSpec(memory_space=pltpu.VMEM)
    dma = pltpu.SemaphoreType.DMA
    results = pl.pallas_call(
        functools.partial(fused_kernel, devices, peers, heads),
        out_shape=(big, big, small, small),
        in_specs=[hbm] * 4,
        out_specs=(vmem,) * 4,
        scratch_shapes=[
            pltpu.VMEM((rows, head_dim), bf16),
            pltpu.VMEM((rows, head_dim), bf16),
            pltpu.VMEM((2, kv_rows, head_dim), bf16),
            pltpu.VMEM((2, kv_rows, head_dim), f32),
            pltpu.VMEM((peers, 2, piece, head_dim), bf16),
            pltpu.VMEM((2, 2 * tokens, head_dim), bf16),
            pltpu.VMEM((2, head_dim, 2 * tokens), bf16),
            pltpu.VMEM((tokens, rows), f32),
            pltpu.VMEM((tokens, rows), f32),
            pltpu.VMEM((8, rows), f32),
            pltpu.VMEM((2 * tokens, rows), bf16),
            pltpu.VMEM((2 * tokens, rows), bf16),
            pltpu.VMEM((2, 2, tokens, head_dim), bf16),
            pltpu.VMEM((2, peers, 2, piece, head_dim), bf16),
            dma((4,)),
            dma((3 * peers,)),
            dma((3 * peers,)),
            dma((4 * peers,)),
            dma((4 * peers,)),
        ],
        compiler_params=pltpu.CompilerParams(
            collective_id=0, has_side_effects=True, vmem_limit_bytes=40 * 1024 * 1024
        ),
    )(
        *(
            pltpu.with_memory_space_constraint(array.reshape(-1, head_dim), pltpu.HBM)
            for array in (queries, key_vectors, value_vectors, out_grad)
        )
    )
    att, dq, dk, dv = pl.pallas_call(
        place_kernel,
        out_shape=(big, big, small, small),
        in_specs=[vmem] * 4,
        out_specs=(hbm,) * 4,
        scratch_shapes=[dma((4,))],
        compiler_params=pltpu.CompilerParams(vmem_limit_bytes=4 * 1024 * 1024),
    )(*results)
    return (
        att.reshape(queries.shape),
        dq.reshape(queries.shape),
        dk.reshape(key_vectors.shape),
        dv.reshape(value_vectors.shape),
    )


def solution(mesh):
    def step(queries, key_vectors, value_vectors, out_grad):
        sizes = (queries.shape[0], queries.shape[1], key_vectors.shape[1], queries.shape[2])
        body = fused_device if pair_groups(mesh.shape["seq"], mesh.shape["head"], sizes) else per_device
        return run(body)(queries, key_vectors, value_vectors, out_grad)

    run = lambda body: jax.shard_map(
        body,
        mesh=mesh,
        in_specs=(
            P("seq", "head", None),
            P(("seq", "head"), None, None),
            P(("seq", "head"), None, None),
            P("seq", "head", None),
        ),
        out_specs=(
            P("seq", "head", None),
            P("seq", "head", None),
            P(("seq", "head"), None, None),
            P(("seq", "head"), None, None),
        ),
        check_vma=False,
    )
    return step
```

```python
import functools
import math

import jax
import jax.numpy as jnp
from jax import lax
from jax.experimental import pallas as pl
from jax.experimental.pallas import tpu as pltpu
from jax.sharding import PartitionSpec as P

GROUPS = 4


def shifted(value, axis, by):
    size = lax.axis_size(axis)
    return lax.ppermute(value, axis, [(i, (i + by) % size) for i in range(size)])


def visible(query_pos, key_pos, group_len, offset, tok_total):
    query_aligned = (query_pos - offset) % tok_total
    key_aligned = (key_pos - offset) % tok_total
    same_group = query_aligned[:, None] // group_len == key_aligned[None, :] // group_len
    return same_group & (key_aligned[None, :] <= query_aligned[:, None])


def per_device(queries, key_vectors, value_vectors, out_grad):
    key_home, value_home = (
        lax.all_to_all(key_vectors, "head", split_axis=1, concat_axis=0, tiled=True),
        lax.all_to_all(value_vectors, "head", split_axis=1, concat_axis=0, tiled=True),
    )
    key_home = key_home[:, 0, :]
    value_home = value_home[:, 0, :]
    tok_rows = queries.shape[0]
    half_heads = queries.shape[1] // 2
    head_dim = queries.shape[2]
    score_scale = 1.0 / math.sqrt(head_dim)
    devices = lax.axis_size("seq")
    group_span = devices // GROUPS
    tok_total = devices * tok_rows
    group_len = tok_total // GROUPS
    offsets = (0, group_len // 2)
    my_index = lax.axis_index("seq")
    local_pos = jnp.arange(tok_rows, dtype=jnp.int32)
    query_pos = my_index * tok_rows + local_pos
    q_parts = (queries[:, :half_heads], queries[:, half_heads:])
    grad_parts = (out_grad[:, :half_heads], out_grad[:, half_heads:])

    def key_positions(distance):
        return (my_index - distance) % devices * tok_rows + local_pos

    def scores_of(which_half, key_blk, allowed):
        scores = (
            jnp.einsum(
                "ihd,td->hit", q_parts[which_half], key_blk, preferred_element_type=jnp.float32
            )
            * score_scale
        )
        return jnp.where(allowed[None], scores, -jnp.inf)

    def forward_tile(states, key_blk, value_blk, distance):
        key_pos = key_positions(distance)
        updated = []
        for which_half in range(2):
            allowed = visible(query_pos, key_pos, group_len, offsets[which_half], tok_total)

            def forward_update(current, which_half=which_half, allowed=allowed):
                run_max, run_sum, running = current
                scores = scores_of(which_half, key_blk, allowed)
                new_max = jnp.maximum(run_max, jnp.max(scores, axis=2))
                weights = jnp.exp(scores - new_max[:, :, None])
                factor = jnp.exp(run_max - new_max)
                run_sum = run_sum * factor + jnp.sum(weights, axis=2)
                value_mix = jnp.einsum(
                    "hit,td->ihd",
                    weights.astype(jnp.bfloat16),
                    value_blk,
                    preferred_element_type=jnp.float32,
                )
                running = running * factor.T[:, :, None] + value_mix
                return (new_max, run_sum, running)

            updated.append(
                lax.cond(
                    jnp.any(allowed), forward_update, lambda current: current, states[which_half]
                )
            )
        return tuple(updated)

    def initial_state():
        return (
            jnp.full((half_heads, tok_rows), -jnp.inf, jnp.float32),
            jnp.zeros((half_heads, tok_rows), jnp.float32),
            jnp.zeros((tok_rows, half_heads, head_dim), jnp.float32),
        )

    forward_init = (initial_state(), initial_state())
    levels = (group_span - 1).bit_length()
    window_keys = key_home[None]
    window_values = value_home[None]
    for level_idx in range(levels):
        far_keys, far_values = shifted((window_keys, window_values), "seq", 2**level_idx)
        window_keys = jnp.concatenate([window_keys, far_keys], axis=0)
        window_values = jnp.concatenate([window_values, far_values], axis=0)

    def window_forward(distance, states):
        return forward_tile(states, window_keys[distance], window_values[distance], distance)

    states = lax.fori_loop(0, group_span, window_forward, forward_init)
    attended_parts = []
    log_totals = []
    deltas = []
    for which_half in range(2):
        run_max, run_sum, running = states[which_half]
        part_out = (running / run_sum.T[:, :, None]).astype(jnp.bfloat16)
        attended_parts.append(part_out)
        log_totals.append(run_max + jnp.log(run_sum))
        deltas.append(
            jnp.einsum(
                "ihd,ihd->hi", grad_parts[which_half], part_out, preferred_element_type=jnp.float32
            )
        )

    def backward_tile(current, key_blk, value_blk, distance):
        query_grads, key_acc, value_acc = current
        key_pos = key_positions(distance)
        new_query = []
        for which_half in range(2):
            allowed = visible(query_pos, key_pos, group_len, offsets[which_half], tok_total)

            def backward_update(inputs, which_half=which_half, allowed=allowed):
                query_acc, key_sum, value_sum = inputs
                scores = scores_of(which_half, key_blk, allowed)
                prob_full = jnp.exp(scores - log_totals[which_half][:, :, None])
                weights = prob_full.astype(jnp.bfloat16)
                prob_grad = jnp.einsum(
                    "ihd,td->hit",
                    grad_parts[which_half],
                    value_blk,
                    preferred_element_type=jnp.float32,
                )
                score_grad = (prob_full * (prob_grad - deltas[which_half][:, :, None])).astype(
                    jnp.bfloat16
                )
                query_acc = query_acc + jnp.einsum(
                    "hit,td->ihd", score_grad, key_blk, preferred_element_type=jnp.float32
                )
                key_sum = key_sum + jnp.einsum(
                    "hit,ihd->td",
                    score_grad,
                    q_parts[which_half],
                    preferred_element_type=jnp.float32,
                )
                value_sum = value_sum + jnp.einsum(
                    "hit,ihd->td",
                    weights,
                    grad_parts[which_half],
                    preferred_element_type=jnp.float32,
                )
                return (query_acc, key_sum, value_sum)

            query_acc, key_acc, value_acc = lax.cond(
                jnp.any(allowed),
                backward_update,
                lambda inputs: inputs,
                (query_grads[which_half], key_acc, value_acc),
            )
            new_query.append(query_acc)
        return (tuple(new_query), key_acc, value_acc)

    zero_query = jnp.zeros((tok_rows, half_heads, head_dim), jnp.float32)
    window_len = 2**levels
    key_buffer = jnp.zeros((window_len, tok_rows, head_dim), jnp.float32)
    value_buffer = jnp.zeros((window_len, tok_rows, head_dim), jnp.float32)

    def window_backward(distance, packed):
        query_grads, key_buffer, value_buffer = packed
        query_grads, key_acc, value_acc = backward_tile(
            (query_grads, key_buffer[distance], value_buffer[distance]),
            window_keys[distance],
            window_values[distance],
            distance,
        )
        key_buffer = lax.dynamic_update_index_in_dim(key_buffer, key_acc, distance, 0)
        value_buffer = lax.dynamic_update_index_in_dim(value_buffer, value_acc, distance, 0)
        return (query_grads, key_buffer, value_buffer)

    query_grads, key_buffer, value_buffer = lax.fori_loop(
        0, group_span, window_backward, ((zero_query, zero_query), key_buffer, value_buffer)
    )
    for level_idx in reversed(range(levels)):
        reach_len = 2**level_idx
        far_keys, far_values = (
            shifted(
                key_buffer[reach_len : 2 * reach_len].astype(jnp.bfloat16), "seq", -reach_len
            ).astype(jnp.float32),
            shifted(
                value_buffer[reach_len : 2 * reach_len].astype(jnp.bfloat16), "seq", -reach_len
            ).astype(jnp.float32),
        )
        key_buffer = key_buffer[:reach_len] + far_keys
        value_buffer = value_buffer[:reach_len] + far_values
    key_acc = key_buffer[0]
    value_acc = value_buffer[0]
    attended = jnp.concatenate(attended_parts, axis=1)
    query_grad = (jnp.concatenate(query_grads, axis=1) * score_scale).astype(jnp.bfloat16)
    key_home_grad = (key_acc * score_scale).astype(jnp.bfloat16)[:, None, :]
    value_home_grad = value_acc.astype(jnp.bfloat16)[:, None, :]
    key_grad, value_grad = (
        lax.all_to_all(key_home_grad, "head", split_axis=0, concat_axis=1, tiled=True),
        lax.all_to_all(value_home_grad, "head", split_axis=0, concat_axis=1, tiled=True),
    )
    return (attended, query_grad, key_grad, value_grad)


def pair_groups(devices, head_devices, sizes):
    _, kv_rows, kv_heads, head_dim = sizes
    return devices == 2 * GROUPS and kv_heads == head_devices and head_dim == 128


NT = (((1,), (1,)), ((), ()))
NN = (((1,), (0,)), ((), ()))


def dot(left, right, dims=NN):
    return lax.dot_general(left, right, dims, preferred_element_type=jnp.float32)


def fused_kernel(
    devices,
    peers,
    heads,
    q_hbm,
    k_hbm,
    v_hbm,
    g_hbm,
    att_ref,
    dq_ref,
    dk_ref,
    dv_ref,
    flat_in,
    flat_out,
    q_ref,
    g_ref,
    kv_in,
    spread,
    kv_send,
    kv,
    kv_t,
    p_own,
    dp_own,
    stats,
    w_ref,
    ds_ref,
    own_sum,
    g_send,
    g_land,
    load_sem,
    kv_send_sem,
    kv_recv_sem,
    g_send_sem,
    g_recv_sem,
):
    s = lax.axis_index("seq")
    h = lax.axis_index("head")
    after = lax.rem(s + 1, devices)
    before = lax.rem(s + devices - 1, devices)
    rows, head_dim = att_ref.shape
    tokens = rows // heads
    piece = tokens // peers
    half = heads // 2
    chunk = 256
    chunk_tok = chunk // half
    chunks = tokens // chunk_tok
    scale = 1.0 / math.sqrt(head_dim)
    unit = scale * 1.4426950408889634
    bases = (lax.rem(s, 2) * half, lax.rem(s + 1, 2) * half)

    def peer(d):
        return lax.rem(h + d, peers)

    raw = ((k_hbm, kv_in.at[0]), (v_hbm, kv_in.at[1]), (q_hbm, att_ref), (g_hbm, dq_ref))
    loads = [pltpu.make_async_copy(src, dst, load_sem.at[i]) for i, (src, dst) in enumerate(raw)]
    for copy in loads:
        copy.start()

    barrier = pltpu.get_barrier_semaphore()
    for d in range(peers):
        pl.semaphore_signal(barrier, inc=1, device_id=(before, peer(d)), device_id_type=MESH)
        if d:
            pl.semaphore_signal(barrier, inc=1, device_id=(s, peer(d)), device_id_type=MESH)

    for which in range(2):
        loads[which].wait()
        spread[which] = kv_in[which].astype(jnp.float32)
        for p in range(peers):
            kv_send[p, which] = spread[which, pl.ds(p, piece, stride=peers), :].astype(jnp.bfloat16)

    mine = pl.ds(pl.multiple_of(h * piece, piece), piece)
    mine_own = pl.ds(pl.multiple_of(tokens + h * piece, piece), piece)
    pl.semaphore_wait(barrier, 2 * peers - 1)

    def send_kv(slot, src, dst, target, d):
        return pltpu.make_async_remote_copy(
            src_ref=src,
            dst_ref=dst,
            send_sem=kv_send_sem.at[slot],
            recv_sem=kv_recv_sem.at[slot],
            device_id=(target, peer(d)),
            device_id_type=MESH,
        )

    own_copies = [
        send_kv(d, kv_send.at[peer(d)], kv.at[:, mine_own, :], s, d) for d in range(1, peers)
    ]
    prev_copies = [
        [
            send_kv(
                (1 + which) * peers + d, kv_send.at[peer(d), which], kv.at[which, mine, :], after, d
            )
            for d in range(peers)
        ]
        for which in range(2)
    ]
    for copy in prev_copies[0] + own_copies + prev_copies[1]:
        copy.start()
    kv[:, mine_own, :] = kv_send[h]

    def head_rows(part, c, j):
        return pl.ds(c * chunk_tok * heads + bases[part] + j, chunk_tok, stride=heads)

    for i, (raw_ref, ref) in enumerate(((att_ref, q_ref), (dq_ref, g_ref))):
        loads[2 + i].wait()
        flat_in[...] = raw_ref[...].astype(jnp.float32)
        for part in range(2):
            for c in range(chunks):
                for j in range(half):
                    low = c * chunk + j * chunk_tok
                    ref[part, low : low + chunk_tok] = flat_in[head_rows(part, c, j), :].astype(
                        jnp.bfloat16
                    )

    for copy in own_copies:
        copy.wait()
    for which in range(2):
        kv_t[which, :, tokens:] = kv[which, tokens:].T

    diag_key = lax.broadcasted_iota(jnp.int32, (chunk_tok, chunk), 0)
    diag_tok = lax.rem(lax.broadcasted_iota(jnp.int32, (chunk_tok, chunk), 1), chunk_tok)
    diag = diag_key <= diag_tok

    def own_tile(part, c):
        here = slice(c * chunk, (c + 1) * chunk)
        own_keys = chunk_tok * (c + 1)
        inner = own_keys - chunk_tok
        scores = dot(kv[0, tokens : tokens + own_keys, :], q_ref[part, here, :], NT) * unit
        edge = jnp.where(diag, scores[inner:], -jnp.inf)
        top = jnp.max(edge, axis=0, keepdims=True)
        if c:
            top = jnp.maximum(top, jnp.max(scores[:inner], axis=0, keepdims=True))
            edge = jnp.concatenate([scores[:inner], edge], axis=0)
        probs = jnp.exp2(edge - top)
        prob_grad = dot(kv[1, tokens : tokens + own_keys, :], g_ref[part, here, :], NT)
        return top, jnp.sum(probs, axis=0, keepdims=True), probs, prob_grad

    def keep(part, c, weights, score_grad):
        here = slice(c * chunk, (c + 1) * chunk)
        top = tokens + chunk_tok * (c + 1)
        limit = tokens + -(-(chunk_tok * (c + 1)) // 128) * 128
        w_ref[part, tokens:top, here] = weights.astype(jnp.bfloat16)
        ds_ref[part, tokens:top, here] = score_grad.astype(jnp.bfloat16)
        if limit > top:
            blank = jnp.zeros((limit - top, chunk), jnp.bfloat16)
            w_ref[part, top:limit, here] = blank
            ds_ref[part, top:limit, here] = blank

    def own_grad(part, which, low):
        keys = slice(tokens + low, tokens + low + 128)
        first = low * half
        left, right = ((ds_ref, q_ref), (w_ref, g_ref))[which]
        return dot(left[part, keys, first:], right[part, first:, :])

    def row_outputs(part, c):
        here = slice(c * chunk, (c + 1) * chunk)
        low = 0 if part else tokens
        limit = tokens + -(-(chunk_tok * (c + 1)) // 128) * 128
        out = dot(kv_t[1, :, low:limit], w_ref[part, low:limit, here])
        grad = dot(kv_t[0, :, low:limit], ds_ref[part, low:limit, here]) * scale
        for i, value in enumerate((out, grad)):
            value = value.astype(jnp.bfloat16).T.astype(jnp.float32)
            for j in range(half):
                flat_out[i, head_rows(part, c, j), :] = value[j * chunk_tok : (j + 1) * chunk_tok]

    for c in range(chunks):
        here = slice(c * chunk, (c + 1) * chunk)
        own_keys = chunk_tok * (c + 1)
        top, total, probs, prob_grad = own_tile(1, c)
        p_own[:own_keys, here] = probs
        dp_own[:own_keys, here] = prob_grad
        stats[0:1, here] = top
        stats[1:2, here] = total
        stats[2:3, here] = jnp.sum(probs * prob_grad, axis=0, keepdims=True)
    for c in range(chunks):
        _, total, probs, prob_grad = own_tile(0, c)
        weights = probs * (1.0 / total)
        delta = jnp.sum(weights * prob_grad, axis=0, keepdims=True)
        keep(0, c, weights, weights * (prob_grad - delta))
    for which in range(2):
        for low in range(0, tokens, 128):
            own_sum[which, low : low + 128] = own_grad(0, which, low)
    for c in range(chunks):
        row_outputs(0, c)

    def send_grads(block, which, slot, target, d):
        return pltpu.make_async_remote_copy(
            src_ref=g_send.at[block, which, pl.ds(pl.multiple_of(peer(d) * piece, piece), piece), :],
            dst_ref=g_land.at[block, h, which],
            send_sem=g_send_sem.at[slot],
            recv_sem=g_recv_sem.at[slot],
            device_id=(target, peer(d)),
            device_id_type=MESH,
        )

    for copy in prev_copies[0]:
        copy.wait()
    for c in range(chunks):
        here = slice(c * chunk, (c + 1) * chunk)
        scores = dot(kv[0, :tokens, :], q_ref[1, here, :], NT) * unit
        top_own = stats[0:1, here]
        top = jnp.maximum(jnp.max(scores, axis=0, keepdims=True), top_own)
        probs = jnp.exp2(scores - top)
        factor = jnp.exp2(top_own - top)
        inverse = 1.0 / (jnp.sum(probs, axis=0, keepdims=True) + factor * stats[1:2, here])
        w_ref[1, :tokens, here] = (probs * inverse).astype(jnp.bfloat16)
        stats[3:4, here] = factor * inverse
    g_send[0, 1] = dot(w_ref[1, :tokens, :], g_ref[1]).astype(jnp.bfloat16)
    prev_v_grads = [send_grads(0, 1, peers + d, before, d) for d in range(peers)]
    for copy in prev_v_grads:
        copy.start()

    for copy in prev_copies[1]:
        copy.wait()
    for c in range(chunks):
        here = slice(c * chunk, (c + 1) * chunk)
        weights = w_ref[1, :tokens, here].astype(jnp.float32)
        prob_grad = dot(kv[1, :tokens, :], g_ref[1, here, :], NT)
        delta = jnp.sum(weights * prob_grad, axis=0, keepdims=True) + stats[3:4, here] * stats[2:3, here]
        stats[4:5, here] = delta
        ds_ref[1, :tokens, here] = (weights * (prob_grad - delta)).astype(jnp.bfloat16)
    g_send[0, 0] = (dot(ds_ref[1, :tokens, :], q_ref[1]) * scale).astype(jnp.bfloat16)
    prev_k_grads = [send_grads(0, 0, d, before, d) for d in range(peers)]
    for copy in prev_k_grads:
        copy.start()

    for c in range(chunks):
        here = slice(c * chunk, (c + 1) * chunk)
        own_keys = chunk_tok * (c + 1)
        weights = p_own[:own_keys, here] * stats[3:4, here]
        keep(1, c, weights, weights * (dp_own[:own_keys, here] - stats[4:5, here]))
    own_grads = []
    for which, factor in ((1, 1.0), (0, scale)):
        for low in range(0, tokens, 128):
            total = own_sum[which, low : low + 128] + own_grad(1, which, low)
            g_send[1, which, low : low + 128] = (total * factor).astype(jnp.bfloat16)
        copies = [send_grads(1, which, (2 + which) * peers + d, s, d) for d in range(1, peers)]
        for copy in copies:
            copy.start()
        own_grads += copies
    g_land[1, h] = g_send[1, :, mine, :]

    for which in range(2):
        kv_t[which, :, :tokens] = kv[which, :tokens].T
    for c in range(chunks):
        row_outputs(1, c)
    att_ref[...] = flat_out[0].astype(jnp.bfloat16)
    dq_ref[...] = flat_out[1].astype(jnp.bfloat16)

    for copy in prev_v_grads + prev_k_grads + own_grads:
        copy.wait()
    for which, out in ((0, dk_ref), (1, dv_ref)):
        for p in range(peers):
            spread[which, pl.ds(p, piece, stride=peers), :] = g_land[0, p, which].astype(
                jnp.float32
            ) + g_land[1, p, which].astype(jnp.float32)
        out[...] = spread[which].astype(jnp.bfloat16)


def place_kernel(*refs):
    count = (len(refs) - 1) // 2
    copies = [
        pltpu.make_async_copy(refs[i], refs[count + i], refs[-1].at[i]) for i in range(count)
    ]
    for copy in copies:
        copy.start()
    for copy in copies:
        copy.wait()


MESH = pl.DeviceIdType.MESH


def fused_device(queries, key_vectors, value_vectors, out_grad):
    devices = lax.axis_size("seq")
    peers = lax.axis_size("head")
    tokens, heads, head_dim = queries.shape
    piece, kv_heads, _ = key_vectors.shape
    rows = tokens * heads
    kv_rows = piece * kv_heads
    bf16, f32 = jnp.bfloat16, jnp.float32
    big = jax.ShapeDtypeStruct((rows, head_dim), bf16)
    small = jax.ShapeDtypeStruct((kv_rows, head_dim), bf16)
    hbm = pl.BlockSpec(memory_space=pltpu.HBM)
    vmem = pl.BlockSpec(memory_space=pltpu.VMEM)
    dma = pltpu.SemaphoreType.DMA
    results = pl.pallas_call(
        functools.partial(fused_kernel, devices, peers, heads),
        out_shape=(big, big, small, small),
        in_specs=[hbm] * 4,
        out_specs=(vmem,) * 4,
        scratch_shapes=[
            pltpu.VMEM((rows, head_dim), f32),
            pltpu.VMEM((2, rows, head_dim), f32),
            pltpu.VMEM((2, rows // 2, head_dim), bf16),
            pltpu.VMEM((2, rows // 2, head_dim), bf16),
            pltpu.VMEM((2, kv_rows, head_dim), bf16),
            pltpu.VMEM((2, kv_rows, head_dim), f32),
            pltpu.VMEM((peers, 2, piece, head_dim), bf16),
            pltpu.VMEM((2, 2 * tokens, head_dim), bf16),
            pltpu.VMEM((2, head_dim, 2 * tokens), bf16),
            pltpu.VMEM((tokens, rows // 2), f32),
            pltpu.VMEM((tokens, rows // 2), f32),
            pltpu.VMEM((8, rows // 2), f32),
            pltpu.VMEM((2, 2 * tokens, rows // 2), bf16),
            pltpu.VMEM((2, 2 * tokens, rows // 2), bf16),
            pltpu.VMEM((2, tokens, head_dim), f32),
            pltpu.VMEM((2, 2, tokens, head_dim), bf16),
            pltpu.VMEM((2, peers, 2, piece, head_dim), bf16),
            dma((4,)),
            dma((3 * peers,)),
            dma((3 * peers,)),
            dma((4 * peers,)),
            dma((4 * peers,)),
        ],
        compiler_params=pltpu.CompilerParams(
            collective_id=0, has_side_effects=True, vmem_limit_bytes=40 * 1024 * 1024
        ),
    )(
        *(
            pltpu.with_memory_space_constraint(array.reshape(-1, head_dim), pltpu.HBM)
            for array in (queries, key_vectors, value_vectors, out_grad)
        )
    )
    att, dq, dk, dv = pl.pallas_call(
        place_kernel,
        out_shape=(big, big, small, small),
        in_specs=[vmem] * 4,
        out_specs=(hbm,) * 4,
        scratch_shapes=[dma((4,))],
        compiler_params=pltpu.CompilerParams(vmem_limit_bytes=4 * 1024 * 1024),
    )(*results)
    return (
        att.reshape(queries.shape),
        dq.reshape(queries.shape),
        dk.reshape(key_vectors.shape),
        dv.reshape(value_vectors.shape),
    )


def solution(mesh):
    def step(queries, key_vectors, value_vectors, out_grad):
        sizes = (queries.shape[0], queries.shape[1], key_vectors.shape[1], queries.shape[2])
        body = fused_device if pair_groups(mesh.shape["seq"], mesh.shape["head"], sizes) else per_device
        return run(body)(queries, key_vectors, value_vectors, out_grad)

    run = lambda body: jax.shard_map(
        body,
        mesh=mesh,
        in_specs=(
            P("seq", "head", None),
            P(("seq", "head"), None, None),
            P(("seq", "head"), None, None),
            P("seq", "head", None),
        ),
        out_specs=(
            P("seq", "head", None),
            P("seq", "head", None),
            P(("seq", "head"), None, None),
            P(("seq", "head"), None, None),
        ),
        check_vma=False,
    )
    return step
```

```python
import functools
import math

import jax
import jax.numpy as jnp
from jax import lax
from jax.experimental import pallas as pl
from jax.experimental.pallas import tpu as pltpu
from jax.sharding import PartitionSpec as P

GROUPS = 4


def shifted(value, axis, by):
    size = lax.axis_size(axis)
    return lax.ppermute(value, axis, [(i, (i + by) % size) for i in range(size)])


def visible(query_pos, key_pos, group_len, offset, tok_total):
    query_aligned = (query_pos - offset) % tok_total
    key_aligned = (key_pos - offset) % tok_total
    same_group = query_aligned[:, None] // group_len == key_aligned[None, :] // group_len
    return same_group & (key_aligned[None, :] <= query_aligned[:, None])


def per_device(queries, key_vectors, value_vectors, out_grad):
    key_home, value_home = (
        lax.all_to_all(key_vectors, "head", split_axis=1, concat_axis=0, tiled=True),
        lax.all_to_all(value_vectors, "head", split_axis=1, concat_axis=0, tiled=True),
    )
    key_home = key_home[:, 0, :]
    value_home = value_home[:, 0, :]
    tok_rows = queries.shape[0]
    half_heads = queries.shape[1] // 2
    head_dim = queries.shape[2]
    score_scale = 1.0 / math.sqrt(head_dim)
    devices = lax.axis_size("seq")
    group_span = devices // GROUPS
    tok_total = devices * tok_rows
    group_len = tok_total // GROUPS
    offsets = (0, group_len // 2)
    my_index = lax.axis_index("seq")
    local_pos = jnp.arange(tok_rows, dtype=jnp.int32)
    query_pos = my_index * tok_rows + local_pos
    q_parts = (queries[:, :half_heads], queries[:, half_heads:])
    grad_parts = (out_grad[:, :half_heads], out_grad[:, half_heads:])

    def key_positions(distance):
        return (my_index - distance) % devices * tok_rows + local_pos

    def scores_of(which_half, key_blk, allowed):
        scores = (
            jnp.einsum(
                "ihd,td->hit", q_parts[which_half], key_blk, preferred_element_type=jnp.float32
            )
            * score_scale
        )
        return jnp.where(allowed[None], scores, -jnp.inf)

    def forward_tile(states, key_blk, value_blk, distance):
        key_pos = key_positions(distance)
        updated = []
        for which_half in range(2):
            allowed = visible(query_pos, key_pos, group_len, offsets[which_half], tok_total)

            def forward_update(current, which_half=which_half, allowed=allowed):
                run_max, run_sum, running = current
                scores = scores_of(which_half, key_blk, allowed)
                new_max = jnp.maximum(run_max, jnp.max(scores, axis=2))
                weights = jnp.exp(scores - new_max[:, :, None])
                factor = jnp.exp(run_max - new_max)
                run_sum = run_sum * factor + jnp.sum(weights, axis=2)
                value_mix = jnp.einsum(
                    "hit,td->ihd",
                    weights.astype(jnp.bfloat16),
                    value_blk,
                    preferred_element_type=jnp.float32,
                )
                running = running * factor.T[:, :, None] + value_mix
                return (new_max, run_sum, running)

            updated.append(
                lax.cond(
                    jnp.any(allowed), forward_update, lambda current: current, states[which_half]
                )
            )
        return tuple(updated)

    def initial_state():
        return (
            jnp.full((half_heads, tok_rows), -jnp.inf, jnp.float32),
            jnp.zeros((half_heads, tok_rows), jnp.float32),
            jnp.zeros((tok_rows, half_heads, head_dim), jnp.float32),
        )

    forward_init = (initial_state(), initial_state())
    levels = (group_span - 1).bit_length()
    window_keys = key_home[None]
    window_values = value_home[None]
    for level_idx in range(levels):
        far_keys, far_values = shifted((window_keys, window_values), "seq", 2**level_idx)
        window_keys = jnp.concatenate([window_keys, far_keys], axis=0)
        window_values = jnp.concatenate([window_values, far_values], axis=0)

    def window_forward(distance, states):
        return forward_tile(states, window_keys[distance], window_values[distance], distance)

    states = lax.fori_loop(0, group_span, window_forward, forward_init)
    attended_parts = []
    log_totals = []
    deltas = []
    for which_half in range(2):
        run_max, run_sum, running = states[which_half]
        part_out = (running / run_sum.T[:, :, None]).astype(jnp.bfloat16)
        attended_parts.append(part_out)
        log_totals.append(run_max + jnp.log(run_sum))
        deltas.append(
            jnp.einsum(
                "ihd,ihd->hi", grad_parts[which_half], part_out, preferred_element_type=jnp.float32
            )
        )

    def backward_tile(current, key_blk, value_blk, distance):
        query_grads, key_acc, value_acc = current
        key_pos = key_positions(distance)
        new_query = []
        for which_half in range(2):
            allowed = visible(query_pos, key_pos, group_len, offsets[which_half], tok_total)

            def backward_update(inputs, which_half=which_half, allowed=allowed):
                query_acc, key_sum, value_sum = inputs
                scores = scores_of(which_half, key_blk, allowed)
                prob_full = jnp.exp(scores - log_totals[which_half][:, :, None])
                weights = prob_full.astype(jnp.bfloat16)
                prob_grad = jnp.einsum(
                    "ihd,td->hit",
                    grad_parts[which_half],
                    value_blk,
                    preferred_element_type=jnp.float32,
                )
                score_grad = (prob_full * (prob_grad - deltas[which_half][:, :, None])).astype(
                    jnp.bfloat16
                )
                query_acc = query_acc + jnp.einsum(
                    "hit,td->ihd", score_grad, key_blk, preferred_element_type=jnp.float32
                )
                key_sum = key_sum + jnp.einsum(
                    "hit,ihd->td",
                    score_grad,
                    q_parts[which_half],
                    preferred_element_type=jnp.float32,
                )
                value_sum = value_sum + jnp.einsum(
                    "hit,ihd->td",
                    weights,
                    grad_parts[which_half],
                    preferred_element_type=jnp.float32,
                )
                return (query_acc, key_sum, value_sum)

            query_acc, key_acc, value_acc = lax.cond(
                jnp.any(allowed),
                backward_update,
                lambda inputs: inputs,
                (query_grads[which_half], key_acc, value_acc),
            )
            new_query.append(query_acc)
        return (tuple(new_query), key_acc, value_acc)

    zero_query = jnp.zeros((tok_rows, half_heads, head_dim), jnp.float32)
    window_len = 2**levels
    key_buffer = jnp.zeros((window_len, tok_rows, head_dim), jnp.float32)
    value_buffer = jnp.zeros((window_len, tok_rows, head_dim), jnp.float32)

    def window_backward(distance, packed):
        query_grads, key_buffer, value_buffer = packed
        query_grads, key_acc, value_acc = backward_tile(
            (query_grads, key_buffer[distance], value_buffer[distance]),
            window_keys[distance],
            window_values[distance],
            distance,
        )
        key_buffer = lax.dynamic_update_index_in_dim(key_buffer, key_acc, distance, 0)
        value_buffer = lax.dynamic_update_index_in_dim(value_buffer, value_acc, distance, 0)
        return (query_grads, key_buffer, value_buffer)

    query_grads, key_buffer, value_buffer = lax.fori_loop(
        0, group_span, window_backward, ((zero_query, zero_query), key_buffer, value_buffer)
    )
    for level_idx in reversed(range(levels)):
        reach_len = 2**level_idx
        far_keys, far_values = (
            shifted(
                key_buffer[reach_len : 2 * reach_len].astype(jnp.bfloat16), "seq", -reach_len
            ).astype(jnp.float32),
            shifted(
                value_buffer[reach_len : 2 * reach_len].astype(jnp.bfloat16), "seq", -reach_len
            ).astype(jnp.float32),
        )
        key_buffer = key_buffer[:reach_len] + far_keys
        value_buffer = value_buffer[:reach_len] + far_values
    key_acc = key_buffer[0]
    value_acc = value_buffer[0]
    attended = jnp.concatenate(attended_parts, axis=1)
    query_grad = (jnp.concatenate(query_grads, axis=1) * score_scale).astype(jnp.bfloat16)
    key_home_grad = (key_acc * score_scale).astype(jnp.bfloat16)[:, None, :]
    value_home_grad = value_acc.astype(jnp.bfloat16)[:, None, :]
    key_grad, value_grad = (
        lax.all_to_all(key_home_grad, "head", split_axis=0, concat_axis=1, tiled=True),
        lax.all_to_all(value_home_grad, "head", split_axis=0, concat_axis=1, tiled=True),
    )
    return (attended, query_grad, key_grad, value_grad)


def pair_groups(devices, head_devices, sizes):
    tokens, heads, kv_heads, head_dim = sizes
    local = tokens // devices
    return (
        devices == 2 * GROUPS
        and kv_heads == head_devices
        and heads == 8 * kv_heads
        and head_devices % 2 == 0
        and head_dim == 128
        and local % 256 == 0
    )


NT = (((1,), (1,)), ((), ()))
NN = (((1,), (0,)), ((), ()))


def dot(left, right, dims=NN):
    return lax.dot_general(left, right, dims, preferred_element_type=jnp.float32)


def fused_kernel(
    devices,
    peers,
    heads,
    q_hbm,
    k_hbm,
    v_hbm,
    g_hbm,
    att_ref,
    dq_ref,
    dk_ref,
    dv_ref,
    flat_in,
    flat_out,
    q_ref,
    g_ref,
    kv_in,
    spread,
    kv_send,
    kv,
    kv_t,
    p_own,
    dp_own,
    stats,
    w_ref,
    ds_ref,
    own_sum,
    g_send,
    g_land,
    load_sem,
    kv_send_sem,
    kv_recv_sem,
    g_send_sem,
    g_recv_sem,
):
    s = lax.axis_index("seq")
    h = lax.axis_index("head")
    after = lax.rem(s + 1, devices)
    before = lax.rem(s + devices - 1, devices)
    rows, head_dim = att_ref.shape
    tokens = rows // heads
    piece = tokens // peers
    half = heads // 2
    chunk = 256
    chunk_tok = chunk // half
    chunks = tokens // chunk_tok
    scale = 1.0 / math.sqrt(head_dim)
    unit = scale * 1.4426950408889634
    bases = (lax.rem(s, 2) * half, lax.rem(s + 1, 2) * half)

    def peer(d):
        return lax.rem(h // 2 + d // 2, peers // 2) * 2 + lax.rem(h + d, 2)

    far_first = [*range(2, peers), *range(2)]

    raw = ((k_hbm, kv_in.at[0]), (v_hbm, kv_in.at[1]), (q_hbm, att_ref), (g_hbm, dq_ref))
    loads = [pltpu.make_async_copy(src, dst, load_sem.at[i]) for i, (src, dst) in enumerate(raw)]
    for copy in loads:
        copy.start()

    barrier = pltpu.get_barrier_semaphore()
    for d in range(peers):
        pl.semaphore_signal(barrier, inc=1, device_id=(before, peer(d)), device_id_type=MESH)
        if d:
            pl.semaphore_signal(barrier, inc=1, device_id=(s, peer(d)), device_id_type=MESH)

    for which in range(2):
        loads[which].wait()
        spread[which] = kv_in[which].astype(jnp.float32)
        for p in range(peers):
            kv_send[p, which] = spread[which, pl.ds(p, piece, stride=peers), :].astype(jnp.bfloat16)

    mine = pl.ds(pl.multiple_of(h * piece, piece), piece)
    mine_own = pl.ds(pl.multiple_of(tokens + h * piece, piece), piece)
    pl.semaphore_wait(barrier, 2 * peers - 1)

    def send_kv(slot, src, dst, target, d):
        return pltpu.make_async_remote_copy(
            src_ref=src,
            dst_ref=dst,
            send_sem=kv_send_sem.at[slot],
            recv_sem=kv_recv_sem.at[slot],
            device_id=(target, peer(d)),
            device_id_type=MESH,
        )

    own_copies = [
        send_kv(d, kv_send.at[peer(d)], kv.at[:, mine_own, :], s, d) for d in far_first if d
    ]
    prev_copies = [
        [
            send_kv(
                (1 + which) * peers + d, kv_send.at[peer(d), which], kv.at[which, mine, :], after, d
            )
            for d in far_first
        ]
        for which in range(2)
    ]
    for copy in prev_copies[0] + own_copies + prev_copies[1]:
        copy.start()
    kv[:, mine_own, :] = kv_send[h]

    def head_rows(part, c, j):
        return pl.ds(c * chunk_tok * heads + bases[part] + j, chunk_tok, stride=heads)

    for i, (raw_ref, ref) in enumerate(((att_ref, q_ref), (dq_ref, g_ref))):
        loads[2 + i].wait()
        flat_in[...] = raw_ref[...].astype(jnp.float32)
        for part in range(2):
            for c in range(chunks):
                for j in range(half):
                    low = c * chunk + j * chunk_tok
                    ref[part, low : low + chunk_tok] = flat_in[head_rows(part, c, j), :].astype(
                        jnp.bfloat16
                    )

    for copy in own_copies:
        copy.wait()
    for which in range(2):
        kv_t[which, :, tokens:] = kv[which, tokens:].T

    diag_key = lax.broadcasted_iota(jnp.int32, (chunk_tok, chunk), 0)
    diag_tok = lax.rem(lax.broadcasted_iota(jnp.int32, (chunk_tok, chunk), 1), chunk_tok)
    diag = diag_key <= diag_tok

    def own_tile(part, c):
        here = slice(c * chunk, (c + 1) * chunk)
        own_keys = chunk_tok * (c + 1)
        inner = own_keys - chunk_tok
        scores = dot(kv[0, tokens : tokens + own_keys, :], q_ref[part, here, :], NT) * unit
        edge = jnp.where(diag, scores[inner:], -jnp.inf)
        top = jnp.max(edge, axis=0, keepdims=True)
        if c:
            top = jnp.maximum(top, jnp.max(scores[:inner], axis=0, keepdims=True))
            edge = jnp.concatenate([scores[:inner], edge], axis=0)
        probs = jnp.exp2(edge - top)
        prob_grad = dot(kv[1, tokens : tokens + own_keys, :], g_ref[part, here, :], NT)
        return top, jnp.sum(probs, axis=0, keepdims=True), probs, prob_grad

    def keep(part, c, weights, score_grad):
        here = slice(c * chunk, (c + 1) * chunk)
        top = tokens + chunk_tok * (c + 1)
        limit = tokens + -(-(chunk_tok * (c + 1)) // 128) * 128
        w_ref[part, tokens:top, here] = weights.astype(jnp.bfloat16)
        ds_ref[part, tokens:top, here] = score_grad.astype(jnp.bfloat16)
        if limit > top:
            blank = jnp.zeros((limit - top, chunk), jnp.bfloat16)
            w_ref[part, top:limit, here] = blank
            ds_ref[part, top:limit, here] = blank

    def own_grad(part, which, low):
        keys = slice(tokens + low, tokens + low + 128)
        first = low * half
        left, right = ((ds_ref, q_ref), (w_ref, g_ref))[which]
        return dot(left[part, keys, first:], right[part, first:, :])

    def row_outputs(part, c):
        here = slice(c * chunk, (c + 1) * chunk)
        low = 0 if part else tokens
        limit = tokens + -(-(chunk_tok * (c + 1)) // 128) * 128
        out = dot(kv_t[1, :, low:limit], w_ref[part, low:limit, here])
        grad = dot(kv_t[0, :, low:limit], ds_ref[part, low:limit, here]) * scale
        for i, value in enumerate((out, grad)):
            value = value.astype(jnp.bfloat16).T.astype(jnp.float32)
            for j in range(half):
                flat_out[i, head_rows(part, c, j), :] = value[j * chunk_tok : (j + 1) * chunk_tok]

    for c in range(chunks):
        here = slice(c * chunk, (c + 1) * chunk)
        own_keys = chunk_tok * (c + 1)
        top, total, probs, prob_grad = own_tile(1, c)
        p_own[:own_keys, here] = probs
        dp_own[:own_keys, here] = prob_grad
        stats[0:1, here] = top
        stats[1:2, here] = total
        stats[2:3, here] = jnp.sum(probs * prob_grad, axis=0, keepdims=True)
    for c in range(chunks):
        _, total, probs, prob_grad = own_tile(0, c)
        weights = probs * (1.0 / total)
        delta = jnp.sum(weights * prob_grad, axis=0, keepdims=True)
        keep(0, c, weights, weights * (prob_grad - delta))
    for which in range(2):
        for low in range(0, tokens, 128):
            own_sum[which, low : low + 128] = own_grad(0, which, low)
    for c in range(chunks):
        row_outputs(0, c)

    def send_grads(block, which, slot, target, d):
        return pltpu.make_async_remote_copy(
            src_ref=g_send.at[block, which, pl.ds(pl.multiple_of(peer(d) * piece, piece), piece), :],
            dst_ref=g_land.at[block, h, which],
            send_sem=g_send_sem.at[slot],
            recv_sem=g_recv_sem.at[slot],
            device_id=(target, peer(d)),
            device_id_type=MESH,
        )

    for copy in prev_copies[0]:
        copy.wait()
    for c in range(chunks):
        here = slice(c * chunk, (c + 1) * chunk)
        scores = dot(kv[0, :tokens, :], q_ref[1, here, :], NT) * unit
        top_own = stats[0:1, here]
        top = jnp.maximum(jnp.max(scores, axis=0, keepdims=True), top_own)
        probs = jnp.exp2(scores - top)
        factor = jnp.exp2(top_own - top)
        inverse = 1.0 / (jnp.sum(probs, axis=0, keepdims=True) + factor * stats[1:2, here])
        w_ref[1, :tokens, here] = (probs * inverse).astype(jnp.bfloat16)
        stats[3:4, here] = factor * inverse
    g_send[0, 1] = dot(w_ref[1, :tokens, :], g_ref[1]).astype(jnp.bfloat16)
    prev_v_grads = [send_grads(0, 1, peers + d, before, d) for d in far_first]
    for copy in prev_v_grads:
        copy.start()

    for copy in prev_copies[1]:
        copy.wait()
    for c in range(chunks):
        here = slice(c * chunk, (c + 1) * chunk)
        weights = w_ref[1, :tokens, here].astype(jnp.float32)
        prob_grad = dot(kv[1, :tokens, :], g_ref[1, here, :], NT)
        delta = jnp.sum(weights * prob_grad, axis=0, keepdims=True) + stats[3:4, here] * stats[2:3, here]
        stats[4:5, here] = delta
        ds_ref[1, :tokens, here] = (weights * (prob_grad - delta)).astype(jnp.bfloat16)
    g_send[0, 0] = (dot(ds_ref[1, :tokens, :], q_ref[1]) * scale).astype(jnp.bfloat16)
    prev_k_grads = [send_grads(0, 0, d, before, d) for d in far_first]
    for copy in prev_k_grads:
        copy.start()

    for c in range(chunks):
        here = slice(c * chunk, (c + 1) * chunk)
        own_keys = chunk_tok * (c + 1)
        weights = p_own[:own_keys, here] * stats[3:4, here]
        keep(1, c, weights, weights * (dp_own[:own_keys, here] - stats[4:5, here]))
    own_grads = []
    for which, factor in ((1, 1.0), (0, scale)):
        for low in range(0, tokens, 128):
            total = own_sum[which, low : low + 128] + own_grad(1, which, low)
            g_send[1, which, low : low + 128] = (total * factor).astype(jnp.bfloat16)
        copies = [send_grads(1, which, (2 + which) * peers + d, s, d) for d in far_first if d]
        for copy in copies:
            copy.start()
        own_grads += copies
    g_land[1, h] = g_send[1, :, mine, :]

    for which in range(2):
        kv_t[which, :, :tokens] = kv[which, :tokens].T
    for c in range(chunks):
        row_outputs(1, c)
    att_ref[...] = flat_out[0].astype(jnp.bfloat16)
    dq_ref[...] = flat_out[1].astype(jnp.bfloat16)

    for copy in prev_v_grads + prev_k_grads + own_grads:
        copy.wait()
    for which, out in ((0, dk_ref), (1, dv_ref)):
        for p in range(peers):
            spread[which, pl.ds(p, piece, stride=peers), :] = g_land[0, p, which].astype(
                jnp.float32
            ) + g_land[1, p, which].astype(jnp.float32)
        out[...] = spread[which].astype(jnp.bfloat16)


def place_kernel(*refs):
    count = (len(refs) - 1) // 2
    copies = [
        pltpu.make_async_copy(refs[i], refs[count + i], refs[-1].at[i]) for i in range(count)
    ]
    for copy in copies:
        copy.start()
    for copy in copies:
        copy.wait()


MESH = pl.DeviceIdType.MESH


def fused_device(queries, key_vectors, value_vectors, out_grad):
    devices = lax.axis_size("seq")
    peers = lax.axis_size("head")
    tokens, heads, head_dim = queries.shape
    piece, kv_heads, _ = key_vectors.shape
    rows = tokens * heads
    kv_rows = piece * kv_heads
    bf16, f32 = jnp.bfloat16, jnp.float32
    big = jax.ShapeDtypeStruct((rows, head_dim), bf16)
    small = jax.ShapeDtypeStruct((kv_rows, head_dim), bf16)
    hbm = pl.BlockSpec(memory_space=pltpu.HBM)
    vmem = pl.BlockSpec(memory_space=pltpu.VMEM)
    dma = pltpu.SemaphoreType.DMA
    results = pl.pallas_call(
        functools.partial(fused_kernel, devices, peers, heads),
        out_shape=(big, big, small, small),
        in_specs=[hbm] * 4,
        out_specs=(vmem,) * 4,
        scratch_shapes=[
            pltpu.VMEM((rows, head_dim), f32),
            pltpu.VMEM((2, rows, head_dim), f32),
            pltpu.VMEM((2, rows // 2, head_dim), bf16),
            pltpu.VMEM((2, rows // 2, head_dim), bf16),
            pltpu.VMEM((2, kv_rows, head_dim), bf16),
            pltpu.VMEM((2, kv_rows, head_dim), f32),
            pltpu.VMEM((peers, 2, piece, head_dim), bf16),
            pltpu.VMEM((2, 2 * tokens, head_dim), bf16),
            pltpu.VMEM((2, head_dim, 2 * tokens), bf16),
            pltpu.VMEM((tokens, rows // 2), f32),
            pltpu.VMEM((tokens, rows // 2), f32),
            pltpu.VMEM((8, rows // 2), f32),
            pltpu.VMEM((2, 2 * tokens, rows // 2), bf16),
            pltpu.VMEM((2, 2 * tokens, rows // 2), bf16),
            pltpu.VMEM((2, tokens, head_dim), f32),
            pltpu.VMEM((2, 2, tokens, head_dim), bf16),
            pltpu.VMEM((2, peers, 2, piece, head_dim), bf16),
            dma((4,)),
            dma((3 * peers,)),
            dma((3 * peers,)),
            dma((4 * peers,)),
            dma((4 * peers,)),
        ],
        compiler_params=pltpu.CompilerParams(
            collective_id=0, has_side_effects=True, vmem_limit_bytes=40 * 1024 * 1024
        ),
    )(
        *(
            pltpu.with_memory_space_constraint(array.reshape(-1, head_dim), pltpu.HBM)
            for array in (queries, key_vectors, value_vectors, out_grad)
        )
    )
    att, dq, dk, dv = pl.pallas_call(
        place_kernel,
        out_shape=(big, big, small, small),
        in_specs=[vmem] * 4,
        out_specs=(hbm,) * 4,
        scratch_shapes=[dma((4,))],
        compiler_params=pltpu.CompilerParams(vmem_limit_bytes=4 * 1024 * 1024),
    )(*results)
    return (
        att.reshape(queries.shape),
        dq.reshape(queries.shape),
        dk.reshape(key_vectors.shape),
        dv.reshape(value_vectors.shape),
    )


def solution(mesh):
    def step(queries, key_vectors, value_vectors, out_grad):
        sizes = (queries.shape[0], queries.shape[1], key_vectors.shape[1], queries.shape[2])
        body = fused_device if pair_groups(mesh.shape["seq"], mesh.shape["head"], sizes) else per_device
        return run(body)(queries, key_vectors, value_vectors, out_grad)

    run = lambda body: jax.shard_map(
        body,
        mesh=mesh,
        in_specs=(
            P("seq", "head", None),
            P(("seq", "head"), None, None),
            P(("seq", "head"), None, None),
            P("seq", "head", None),
        ),
        out_specs=(
            P("seq", "head", None),
            P("seq", "head", None),
            P(("seq", "head"), None, None),
            P(("seq", "head"), None, None),
        ),
        check_vma=False,
    )
    return step
```

```python
import functools
import math

import jax
import jax.numpy as jnp
from jax import lax
from jax.experimental import pallas as pl
from jax.experimental.pallas import tpu as pltpu
from jax.sharding import PartitionSpec as P

GROUPS = 4


def shifted(value, axis, by):
    size = lax.axis_size(axis)
    return lax.ppermute(value, axis, [(i, (i + by) % size) for i in range(size)])


def visible(query_pos, key_pos, group_len, offset, tok_total):
    query_aligned = (query_pos - offset) % tok_total
    key_aligned = (key_pos - offset) % tok_total
    same_group = query_aligned[:, None] // group_len == key_aligned[None, :] // group_len
    return same_group & (key_aligned[None, :] <= query_aligned[:, None])


def per_device(queries, key_vectors, value_vectors, out_grad):
    key_home, value_home = (
        lax.all_to_all(key_vectors, "head", split_axis=1, concat_axis=0, tiled=True),
        lax.all_to_all(value_vectors, "head", split_axis=1, concat_axis=0, tiled=True),
    )
    key_home = key_home[:, 0, :]
    value_home = value_home[:, 0, :]
    tok_rows = queries.shape[0]
    half_heads = queries.shape[1] // 2
    head_dim = queries.shape[2]
    score_scale = 1.0 / math.sqrt(head_dim)
    devices = lax.axis_size("seq")
    group_span = devices // GROUPS
    tok_total = devices * tok_rows
    group_len = tok_total // GROUPS
    offsets = (0, group_len // 2)
    my_index = lax.axis_index("seq")
    local_pos = jnp.arange(tok_rows, dtype=jnp.int32)
    query_pos = my_index * tok_rows + local_pos
    q_parts = (queries[:, :half_heads], queries[:, half_heads:])
    grad_parts = (out_grad[:, :half_heads], out_grad[:, half_heads:])

    def key_positions(distance):
        return (my_index - distance) % devices * tok_rows + local_pos

    def scores_of(which_half, key_blk, allowed):
        scores = (
            jnp.einsum(
                "ihd,td->hit", q_parts[which_half], key_blk, preferred_element_type=jnp.float32
            )
            * score_scale
        )
        return jnp.where(allowed[None], scores, -jnp.inf)

    def forward_tile(states, key_blk, value_blk, distance):
        key_pos = key_positions(distance)
        updated = []
        for which_half in range(2):
            allowed = visible(query_pos, key_pos, group_len, offsets[which_half], tok_total)

            def forward_update(current, which_half=which_half, allowed=allowed):
                run_max, run_sum, running = current
                scores = scores_of(which_half, key_blk, allowed)
                new_max = jnp.maximum(run_max, jnp.max(scores, axis=2))
                weights = jnp.exp(scores - new_max[:, :, None])
                factor = jnp.exp(run_max - new_max)
                run_sum = run_sum * factor + jnp.sum(weights, axis=2)
                value_mix = jnp.einsum(
                    "hit,td->ihd",
                    weights.astype(jnp.bfloat16),
                    value_blk,
                    preferred_element_type=jnp.float32,
                )
                running = running * factor.T[:, :, None] + value_mix
                return (new_max, run_sum, running)

            updated.append(
                lax.cond(
                    jnp.any(allowed), forward_update, lambda current: current, states[which_half]
                )
            )
        return tuple(updated)

    def initial_state():
        return (
            jnp.full((half_heads, tok_rows), -jnp.inf, jnp.float32),
            jnp.zeros((half_heads, tok_rows), jnp.float32),
            jnp.zeros((tok_rows, half_heads, head_dim), jnp.float32),
        )

    forward_init = (initial_state(), initial_state())
    levels = (group_span - 1).bit_length()
    window_keys = key_home[None]
    window_values = value_home[None]
    for level_idx in range(levels):
        far_keys, far_values = shifted((window_keys, window_values), "seq", 2**level_idx)
        window_keys = jnp.concatenate([window_keys, far_keys], axis=0)
        window_values = jnp.concatenate([window_values, far_values], axis=0)

    def window_forward(distance, states):
        return forward_tile(states, window_keys[distance], window_values[distance], distance)

    states = lax.fori_loop(0, group_span, window_forward, forward_init)
    attended_parts = []
    log_totals = []
    deltas = []
    for which_half in range(2):
        run_max, run_sum, running = states[which_half]
        part_out = (running / run_sum.T[:, :, None]).astype(jnp.bfloat16)
        attended_parts.append(part_out)
        log_totals.append(run_max + jnp.log(run_sum))
        deltas.append(
            jnp.einsum(
                "ihd,ihd->hi", grad_parts[which_half], part_out, preferred_element_type=jnp.float32
            )
        )

    def backward_tile(current, key_blk, value_blk, distance):
        query_grads, key_acc, value_acc = current
        key_pos = key_positions(distance)
        new_query = []
        for which_half in range(2):
            allowed = visible(query_pos, key_pos, group_len, offsets[which_half], tok_total)

            def backward_update(inputs, which_half=which_half, allowed=allowed):
                query_acc, key_sum, value_sum = inputs
                scores = scores_of(which_half, key_blk, allowed)
                prob_full = jnp.exp(scores - log_totals[which_half][:, :, None])
                weights = prob_full.astype(jnp.bfloat16)
                prob_grad = jnp.einsum(
                    "ihd,td->hit",
                    grad_parts[which_half],
                    value_blk,
                    preferred_element_type=jnp.float32,
                )
                score_grad = (prob_full * (prob_grad - deltas[which_half][:, :, None])).astype(
                    jnp.bfloat16
                )
                query_acc = query_acc + jnp.einsum(
                    "hit,td->ihd", score_grad, key_blk, preferred_element_type=jnp.float32
                )
                key_sum = key_sum + jnp.einsum(
                    "hit,ihd->td",
                    score_grad,
                    q_parts[which_half],
                    preferred_element_type=jnp.float32,
                )
                value_sum = value_sum + jnp.einsum(
                    "hit,ihd->td",
                    weights,
                    grad_parts[which_half],
                    preferred_element_type=jnp.float32,
                )
                return (query_acc, key_sum, value_sum)

            query_acc, key_acc, value_acc = lax.cond(
                jnp.any(allowed),
                backward_update,
                lambda inputs: inputs,
                (query_grads[which_half], key_acc, value_acc),
            )
            new_query.append(query_acc)
        return (tuple(new_query), key_acc, value_acc)

    zero_query = jnp.zeros((tok_rows, half_heads, head_dim), jnp.float32)
    window_len = 2**levels
    key_buffer = jnp.zeros((window_len, tok_rows, head_dim), jnp.float32)
    value_buffer = jnp.zeros((window_len, tok_rows, head_dim), jnp.float32)

    def window_backward(distance, packed):
        query_grads, key_buffer, value_buffer = packed
        query_grads, key_acc, value_acc = backward_tile(
            (query_grads, key_buffer[distance], value_buffer[distance]),
            window_keys[distance],
            window_values[distance],
            distance,
        )
        key_buffer = lax.dynamic_update_index_in_dim(key_buffer, key_acc, distance, 0)
        value_buffer = lax.dynamic_update_index_in_dim(value_buffer, value_acc, distance, 0)
        return (query_grads, key_buffer, value_buffer)

    query_grads, key_buffer, value_buffer = lax.fori_loop(
        0, group_span, window_backward, ((zero_query, zero_query), key_buffer, value_buffer)
    )
    for level_idx in reversed(range(levels)):
        reach_len = 2**level_idx
        far_keys, far_values = (
            shifted(
                key_buffer[reach_len : 2 * reach_len].astype(jnp.bfloat16), "seq", -reach_len
            ).astype(jnp.float32),
            shifted(
                value_buffer[reach_len : 2 * reach_len].astype(jnp.bfloat16), "seq", -reach_len
            ).astype(jnp.float32),
        )
        key_buffer = key_buffer[:reach_len] + far_keys
        value_buffer = value_buffer[:reach_len] + far_values
    key_acc = key_buffer[0]
    value_acc = value_buffer[0]
    attended = jnp.concatenate(attended_parts, axis=1)
    query_grad = (jnp.concatenate(query_grads, axis=1) * score_scale).astype(jnp.bfloat16)
    key_home_grad = (key_acc * score_scale).astype(jnp.bfloat16)[:, None, :]
    value_home_grad = value_acc.astype(jnp.bfloat16)[:, None, :]
    key_grad, value_grad = (
        lax.all_to_all(key_home_grad, "head", split_axis=0, concat_axis=1, tiled=True),
        lax.all_to_all(value_home_grad, "head", split_axis=0, concat_axis=1, tiled=True),
    )
    return (attended, query_grad, key_grad, value_grad)


def pair_groups(devices, head_devices, sizes):
    tokens, heads, kv_heads, head_dim = sizes
    local = tokens // devices
    return (
        devices == 2 * GROUPS
        and kv_heads == head_devices
        and heads == 8 * kv_heads
        and head_devices % 2 == 0
        and head_dim == 128
        and local % 256 == 0
    )


NT = (((1,), (1,)), ((), ()))
NN = (((1,), (0,)), ((), ()))


def dot(left, right, dims=NN):
    return lax.dot_general(left, right, dims, preferred_element_type=jnp.float32)


def fused_kernel(
    devices,
    peers,
    heads,
    q_hbm,
    k_hbm,
    v_hbm,
    g_hbm,
    att_ref,
    dq_ref,
    dk_ref,
    dv_ref,
    flat_in,
    flat_out,
    q_ref,
    g_ref,
    kv_in,
    spread,
    kv_send,
    kv,
    kv_t,
    p_own,
    dp_own,
    stats,
    w_ref,
    ds_ref,
    own_sum,
    g_send,
    g_land,
    load_sem,
    kv_send_sem,
    kv_recv_sem,
    g_send_sem,
    g_recv_sem,
):
    s = lax.axis_index("seq")
    h = lax.axis_index("head")
    after = lax.rem(s + 1, devices)
    before = lax.rem(s + devices - 1, devices)
    rows, head_dim = att_ref.shape
    tokens = rows // heads
    piece = tokens // peers
    half = heads // 2
    chunk = 256
    chunk_tok = chunk // half
    chunks = tokens // chunk_tok
    scale = 1.0 / math.sqrt(head_dim)
    unit = scale * 1.4426950408889634
    bases = (lax.rem(s, 2) * half, lax.rem(s + 1, 2) * half)

    def peer(d):
        return lax.rem(h // 2 + d // 2, peers // 2) * 2 + lax.rem(h + d, 2)

    far_first = [*range(2, peers), *range(2)]

    raw = ((k_hbm, kv_in.at[0]), (v_hbm, kv_in.at[1]), (q_hbm, att_ref), (g_hbm, dq_ref))
    loads = [pltpu.make_async_copy(src, dst, load_sem.at[i]) for i, (src, dst) in enumerate(raw)]
    for copy in loads:
        copy.start()

    barrier = pltpu.get_barrier_semaphore()
    for d in range(peers):
        pl.semaphore_signal(barrier, inc=1, device_id=(before, peer(d)), device_id_type=MESH)
        if d:
            pl.semaphore_signal(barrier, inc=1, device_id=(s, peer(d)), device_id_type=MESH)

    for which in range(2):
        loads[which].wait()
        spread[which] = kv_in[which].astype(jnp.float32)
        for p in range(peers):
            kv_send[p, which] = spread[which, pl.ds(p, piece, stride=peers), :].astype(jnp.bfloat16)

    mine = pl.ds(pl.multiple_of(h * piece, piece), piece)
    mine_own = pl.ds(pl.multiple_of(tokens + h * piece, piece), piece)
    pl.semaphore_wait(barrier, 2 * peers - 1)

    def send_kv(slot, src, dst, target, d):
        return pltpu.make_async_remote_copy(
            src_ref=src,
            dst_ref=dst,
            send_sem=kv_send_sem.at[slot],
            recv_sem=kv_recv_sem.at[slot],
            device_id=(target, peer(d)),
            device_id_type=MESH,
        )

    own_copies = [
        send_kv(d, kv_send.at[peer(d)], kv.at[:, mine_own, :], s, d) for d in far_first if d
    ]
    prev_copies = [
        [
            send_kv(
                (1 + which) * peers + d, kv_send.at[peer(d), which], kv.at[which, mine, :], after, d
            )
            for d in far_first
        ]
        for which in range(2)
    ]
    for copy in prev_copies[0] + own_copies + prev_copies[1]:
        copy.start()
    kv[:, mine_own, :] = kv_send[h]

    def head_rows(part, c, j):
        return pl.ds(c * chunk_tok * heads + bases[part] + j, chunk_tok, stride=heads)

    for i, (raw_ref, ref) in enumerate(((att_ref, q_ref), (dq_ref, g_ref))):
        loads[2 + i].wait()
        flat_in[...] = raw_ref[...].astype(jnp.float32)
        for part in range(2):
            for c in range(chunks):
                for j in range(half):
                    low = c * chunk + j * chunk_tok
                    ref[part, low : low + chunk_tok] = flat_in[head_rows(part, c, j), :].astype(
                        jnp.bfloat16
                    )

    for copy in own_copies:
        copy.wait()
    for which in range(2):
        kv_t[which, :, tokens:] = kv[which, tokens:].T

    diag_key = lax.broadcasted_iota(jnp.int32, (chunk_tok, chunk), 0)
    diag_tok = lax.rem(lax.broadcasted_iota(jnp.int32, (chunk_tok, chunk), 1), chunk_tok)
    diag = diag_key <= diag_tok

    def own_tile(part, c):
        here = slice(c * chunk, (c + 1) * chunk)
        own_keys = chunk_tok * (c + 1)
        inner = own_keys - chunk_tok
        scores = dot(kv[0, tokens : tokens + own_keys, :], q_ref[part, here, :], NT) * unit
        edge = jnp.where(diag, scores[inner:], -jnp.inf)
        top = jnp.max(edge, axis=0, keepdims=True)
        if c:
            top = jnp.maximum(top, jnp.max(scores[:inner], axis=0, keepdims=True))
            edge = jnp.concatenate([scores[:inner], edge], axis=0)
        probs = jnp.exp2(edge - top)
        prob_grad = dot(kv[1, tokens : tokens + own_keys, :], g_ref[part, here, :], NT)
        return top, jnp.sum(probs, axis=0, keepdims=True), probs, prob_grad

    def keep(part, c, weights, score_grad):
        here = slice(c * chunk, (c + 1) * chunk)
        top = tokens + chunk_tok * (c + 1)
        limit = tokens + -(-(chunk_tok * (c + 1)) // 128) * 128
        w_ref[part, tokens:top, here] = weights.astype(jnp.bfloat16)
        ds_ref[part, tokens:top, here] = score_grad.astype(jnp.bfloat16)
        if limit > top:
            blank = jnp.zeros((limit - top, chunk), jnp.bfloat16)
            w_ref[part, top:limit, here] = blank
            ds_ref[part, top:limit, here] = blank

    def own_grad(part, which, low):
        keys = slice(tokens + low, tokens + low + 128)
        first = low * half
        left, right = ((ds_ref, q_ref), (w_ref, g_ref))[which]
        return dot(left[part, keys, first:], right[part, first:, :])

    def row_outputs(part, c):
        here = slice(c * chunk, (c + 1) * chunk)
        low = 0 if part else tokens
        limit = tokens + -(-(chunk_tok * (c + 1)) // 128) * 128
        out = dot(kv_t[1, :, low:limit], w_ref[part, low:limit, here])
        grad = dot(kv_t[0, :, low:limit], ds_ref[part, low:limit, here]) * scale
        for i, value in enumerate((out, grad)):
            value = value.astype(jnp.bfloat16).T.astype(jnp.float32)
            for j in range(half):
                flat_out[i, head_rows(part, c, j), :] = value[j * chunk_tok : (j + 1) * chunk_tok]

    for c in range(chunks):
        here = slice(c * chunk, (c + 1) * chunk)
        own_keys = chunk_tok * (c + 1)
        top, total, probs, prob_grad = own_tile(1, c)
        p_own[:own_keys, here] = probs
        dp_own[:own_keys, here] = prob_grad
        stats[0:1, here] = top
        stats[1:2, here] = total
        stats[2:3, here] = jnp.sum(probs * prob_grad, axis=0, keepdims=True)
    for c in range(chunks):
        _, total, probs, prob_grad = own_tile(0, c)
        weights = probs * (1.0 / total)
        delta = jnp.sum(weights * prob_grad, axis=0, keepdims=True)
        keep(0, c, weights, weights * (prob_grad - delta))
    for which in range(2):
        for low in range(0, tokens, 128):
            own_sum[which, low : low + 128] = own_grad(0, which, low)
    for c in range(chunks):
        row_outputs(0, c)

    def send_grads(block, which, slot, target, d):
        return pltpu.make_async_remote_copy(
            src_ref=g_send.at[block, which, pl.ds(pl.multiple_of(peer(d) * piece, piece), piece), :],
            dst_ref=g_land.at[block, h, which],
            send_sem=g_send_sem.at[slot],
            recv_sem=g_recv_sem.at[slot],
            device_id=(target, peer(d)),
            device_id_type=MESH,
        )

    for copy in prev_copies[0]:
        copy.wait()
    for c in range(chunks):
        here = slice(c * chunk, (c + 1) * chunk)
        scores = dot(kv[0, :tokens, :], q_ref[1, here, :], NT) * unit
        top_own = stats[0:1, here]
        top = jnp.maximum(jnp.max(scores, axis=0, keepdims=True), top_own)
        probs = jnp.exp2(scores - top)
        factor = jnp.exp2(top_own - top)
        inverse = 1.0 / (jnp.sum(probs, axis=0, keepdims=True) + factor * stats[1:2, here])
        w_ref[1, :tokens, here] = (probs * inverse).astype(jnp.bfloat16)
        stats[3:4, here] = factor * inverse
    g_send[0, 1] = dot(w_ref[1, :tokens, :], g_ref[1]).astype(jnp.bfloat16)
    prev_v_grads = [send_grads(0, 1, peers + d, before, d) for d in far_first]
    for copy in prev_v_grads:
        copy.start()

    for copy in prev_copies[1]:
        copy.wait()
    for c in range(chunks):
        here = slice(c * chunk, (c + 1) * chunk)
        weights = w_ref[1, :tokens, here].astype(jnp.float32)
        prob_grad = dot(kv[1, :tokens, :], g_ref[1, here, :], NT)
        delta = jnp.sum(weights * prob_grad, axis=0, keepdims=True) + stats[3:4, here] * stats[2:3, here]
        stats[4:5, here] = delta
        ds_ref[1, :tokens, here] = (weights * (prob_grad - delta)).astype(jnp.bfloat16)
    g_send[0, 0] = (dot(ds_ref[1, :tokens, :], q_ref[1]) * scale).astype(jnp.bfloat16)
    prev_k_grads = [send_grads(0, 0, d, before, d) for d in far_first]
    for copy in prev_k_grads:
        copy.start()

    for c in range(chunks):
        here = slice(c * chunk, (c + 1) * chunk)
        own_keys = chunk_tok * (c + 1)
        weights = p_own[:own_keys, here] * stats[3:4, here]
        keep(1, c, weights, weights * (dp_own[:own_keys, here] - stats[4:5, here]))
    own_grads = []
    for which, factor in ((1, 1.0), (0, scale)):
        for low in range(0, tokens, 128):
            total = own_sum[which, low : low + 128] + own_grad(1, which, low)
            g_send[1, which, low : low + 128] = (total * factor).astype(jnp.bfloat16)
        copies = [send_grads(1, which, (2 + which) * peers + d, s, d) for d in far_first if d]
        for copy in copies:
            copy.start()
        own_grads += copies
    g_land[1, h] = g_send[1, :, mine, :]

    for which in range(2):
        kv_t[which, :, :tokens] = kv[which, :tokens].T
    for c in range(chunks):
        row_outputs(1, c)
    att_ref[...] = flat_out[0].astype(jnp.bfloat16)
    dq_ref[...] = flat_out[1].astype(jnp.bfloat16)

    for copy in prev_v_grads + prev_k_grads + own_grads:
        copy.wait_recv()
    for which, out in ((0, dk_ref), (1, dv_ref)):
        for p in range(peers):
            spread[which, pl.ds(p, piece, stride=peers), :] = g_land[0, p, which].astype(
                jnp.float32
            ) + g_land[1, p, which].astype(jnp.float32)
        out[...] = spread[which].astype(jnp.bfloat16)
    for copy in prev_v_grads + prev_k_grads + own_grads:
        copy.wait_send()


def place_kernel(*refs):
    count = (len(refs) - 1) // 2
    copies = [
        pltpu.make_async_copy(refs[i], refs[count + i], refs[-1].at[i]) for i in range(count)
    ]
    for copy in copies:
        copy.start()
    for copy in copies:
        copy.wait()


MESH = pl.DeviceIdType.MESH


def fused_device(queries, key_vectors, value_vectors, out_grad):
    devices = lax.axis_size("seq")
    peers = lax.axis_size("head")
    tokens, heads, head_dim = queries.shape
    piece, kv_heads, _ = key_vectors.shape
    rows = tokens * heads
    kv_rows = piece * kv_heads
    bf16, f32 = jnp.bfloat16, jnp.float32
    big = jax.ShapeDtypeStruct((rows, head_dim), bf16)
    small = jax.ShapeDtypeStruct((kv_rows, head_dim), bf16)
    hbm = pl.BlockSpec(memory_space=pltpu.HBM)
    vmem = pl.BlockSpec(memory_space=pltpu.VMEM)
    dma = pltpu.SemaphoreType.DMA
    results = pl.pallas_call(
        functools.partial(fused_kernel, devices, peers, heads),
        out_shape=(big, big, small, small),
        in_specs=[hbm] * 4,
        out_specs=(vmem,) * 4,
        scratch_shapes=[
            pltpu.VMEM((rows, head_dim), f32),
            pltpu.VMEM((2, rows, head_dim), f32),
            pltpu.VMEM((2, rows // 2, head_dim), bf16),
            pltpu.VMEM((2, rows // 2, head_dim), bf16),
            pltpu.VMEM((2, kv_rows, head_dim), bf16),
            pltpu.VMEM((2, kv_rows, head_dim), f32),
            pltpu.VMEM((peers, 2, piece, head_dim), bf16),
            pltpu.VMEM((2, 2 * tokens, head_dim), bf16),
            pltpu.VMEM((2, head_dim, 2 * tokens), bf16),
            pltpu.VMEM((tokens, rows // 2), f32),
            pltpu.VMEM((tokens, rows // 2), f32),
            pltpu.VMEM((8, rows // 2), f32),
            pltpu.VMEM((2, 2 * tokens, rows // 2), bf16),
            pltpu.VMEM((2, 2 * tokens, rows // 2), bf16),
            pltpu.VMEM((2, tokens, head_dim), f32),
            pltpu.VMEM((2, 2, tokens, head_dim), bf16),
            pltpu.VMEM((2, peers, 2, piece, head_dim), bf16),
            dma((4,)),
            dma((3 * peers,)),
            dma((3 * peers,)),
            dma((4 * peers,)),
            dma((4 * peers,)),
        ],
        compiler_params=pltpu.CompilerParams(
            collective_id=0, has_side_effects=True, vmem_limit_bytes=40 * 1024 * 1024
        ),
    )(
        *(
            pltpu.with_memory_space_constraint(array.reshape(-1, head_dim), pltpu.HBM)
            for array in (queries, key_vectors, value_vectors, out_grad)
        )
    )
    att, dq, dk, dv = pl.pallas_call(
        place_kernel,
        out_shape=(big, big, small, small),
        in_specs=[vmem] * 4,
        out_specs=(hbm,) * 4,
        scratch_shapes=[dma((4,))],
        compiler_params=pltpu.CompilerParams(vmem_limit_bytes=4 * 1024 * 1024),
    )(*results)
    return (
        att.reshape(queries.shape),
        dq.reshape(queries.shape),
        dk.reshape(key_vectors.shape),
        dv.reshape(value_vectors.shape),
    )


def solution(mesh):
    def step(queries, key_vectors, value_vectors, out_grad):
        sizes = (queries.shape[0], queries.shape[1], key_vectors.shape[1], queries.shape[2])
        body = fused_device if pair_groups(mesh.shape["seq"], mesh.shape["head"], sizes) else per_device
        return run(body)(queries, key_vectors, value_vectors, out_grad)

    run = lambda body: jax.shard_map(
        body,
        mesh=mesh,
        in_specs=(
            P("seq", "head", None),
            P(("seq", "head"), None, None),
            P(("seq", "head"), None, None),
            P("seq", "head", None),
        ),
        out_specs=(
            P("seq", "head", None),
            P("seq", "head", None),
            P(("seq", "head"), None, None),
            P(("seq", "head"), None, None),
        ),
        check_vma=False,
    )
    return step
```
